256 devices in a mesh: gx: 8 (over y, x_lo), gy: 2 (over x_hi), vert: 16 (over z, core).
Axes of the slice: x: 4 (x_hi: 2, x_lo: 2; x = x_hi * 2 + x_lo), y: 4, z: 8, core: 2. Of those that a mesh axis runs over, the one named last changes fastest.
Arguments:
- state: float32 [8000, 3, 4, 1024], P('vert', None, 'gy', 'gx'), as said below
- tangent: float32 [8000, 3, 4, 1024], P('vert', None, 'gy', 'gx')
- orient: int32 [8000, 2], P('vert'), may hold values from 0 to 1, as said below
- walls: int32 [2, 1024], P(None, 'gx'), may hold values from 0 to 1
Outputs:
- product: float32 [8000, 3, 4, 1024], P('vert', None, 'gy', 'gx')
The draws below stay inside these ranges and needn't reach their ends.
Inputs may be any that keep to these rules, and one draw needn't show every extreme that they name: In every aligned group of four slots 4k to 4k+3 there are two bits p, r with orient[4k + 2b + e] = (e XOR p, b XOR r) for b, e in 0, 1. The state's values at the four points q of every cell are positive.
All inputs are finite; a program needn't handle non-finite values.
Results may differ from the reference program's by a relative error of at most 0.0003.
Values sent between devices are 32-bit elements; how exact they have to be, the bound alone decides.
A program may use at most 64 MiB of HBM per device.

```python
import math
import jax
import jax.numpy as jnp
from jax import lax

NVX = 20
NV = 8000
STREAMWISE_SLABS = 1024
CROSSWISE_SLABS = 4


def draw_state(key, part):
    half_grid = NVX // 2
    spacing = 5.0 / half_grid
    noise_seedlets = jax.random.split(key, 6)
    slot_index = jnp.arange(NV, dtype=jnp.int32)
    mag_x = (slot_index // (4 * half_grid) % half_grid).astype(jnp.float32) + 0.5
    mag_y = (slot_index // 4 % half_grid).astype(jnp.float32) + 0.5
    level_z = (slot_index // (4 * half_grid * half_grid)).astype(jnp.float32) - (half_grid - 0.5)
    stream_magnitude = ((mag_x * spacing) ** 2 + (mag_y * spacing) ** 2).reshape(NV, 1, 1)
    molecular_grid_extent = (level_z * spacing).reshape(NV, 1, 1)
    thermal_bottom_plate, thermal_roof_plate, jitter_floor, jitter_ceiling, gradient_clamp = (0.7, 1.4, 0.5, 1.5, 0.4)
    thermal_state = jnp.exp(jax.random.uniform(noise_seedlets[0], (1, CROSSWISE_SLABS, STREAMWISE_SLABS), jnp.float32, math.log(thermal_bottom_plate), math.log(thermal_roof_plate)))
    average_offset = jax.random.uniform(noise_seedlets[1], (1, CROSSWISE_SLABS, STREAMWISE_SLABS), jnp.float32, -0.5, 0.5)
    reference_height = jnp.exp(jax.random.uniform(noise_seedlets[2], (1, CROSSWISE_SLABS, STREAMWISE_SLABS), jnp.float32, math.log(0.5), math.log(2.0)))
    streamwise_shape = reference_height * jnp.exp(-(stream_magnitude + (molecular_grid_extent - average_offset) ** 2) / (2.0 * thermal_state)) / (2.0 * math.pi * thermal_state) ** 1.5
    mean_part = streamwise_shape * jax.random.uniform(noise_seedlets[3], (NV, CROSSWISE_SLABS, STREAMWISE_SLABS), jnp.float32, jitter_floor, jitter_ceiling)
    slope_x = mean_part * jax.random.uniform(noise_seedlets[4], (NV, CROSSWISE_SLABS, STREAMWISE_SLABS), jnp.float32, -gradient_clamp, gradient_clamp)
    slope_y = mean_part * jax.random.uniform(noise_seedlets[5], (NV, CROSSWISE_SLABS, STREAMWISE_SLABS), jnp.float32, -gradient_clamp, gradient_clamp)
    return jnp.stack([mean_part, slope_x, slope_y], axis=1)


def draw_tangent(key, part):
    noise_seedlets = jax.random.split(key, 3)
    vel_scale = jnp.exp(jax.random.uniform(noise_seedlets[0], (NV, 1, 1, 1), jnp.float32, math.log(0.1), math.log(1.0)))
    cell_scale = jnp.exp(jax.random.uniform(noise_seedlets[1], (1, 1, CROSSWISE_SLABS, STREAMWISE_SLABS), jnp.float32, math.log(0.3), math.log(3.0)))
    base_draw = jax.random.truncated_normal(noise_seedlets[2], -4.0, 4.0, (NV, 3, CROSSWISE_SLABS, STREAMWISE_SLABS), jnp.float32)
    return base_draw * vel_scale * cell_scale


def draw_orient(key, part):
    flip_bits = jax.random.randint(key, (NV // 4, 2), 0, 2, dtype=jnp.int32)
    slot_index = jnp.arange(NV, dtype=jnp.int32)
    group_index = slot_index // 4
    sign_x = (slot_index % 2 + flip_bits[group_index, 0]) % 2
    sign_y = (slot_index // 2 % 2 + flip_bits[group_index, 1]) % 2
    return jnp.stack([sign_x, sign_y], axis=1).astype(jnp.int32)


def with_ends(values, stream_key, smallest, largest):
    extent = values.shape
    index_at = [jax.random.randint(jax.random.fold_in(stream_key, axis), (), 0, extent[axis]) for axis in range(len(extent))]
    values = values.at[tuple(index_at)].set(smallest)
    longest = extent.index(max(extent))
    index_at[longest] = (index_at[longest] + 1) % extent[longest]
    return values.at[tuple(index_at)].set(largest)


def setup_inputs(seed: int = 0) -> dict:
    key_of = jax.random.split(jax.random.key(seed), 5)
    state = draw_state(jax.random.fold_in(key_of[4], 71), 0)
    tangent = draw_tangent(jax.random.fold_in(key_of[4], 71), 0)
    orient = draw_orient(jax.random.fold_in(key_of[4], 71), 0)
    walls = with_ends(jax.random.randint(key_of[3], (2, STREAMWISE_SLABS), 0, 2), jax.random.fold_in(key_of[3], 1), 0, 1).astype(jnp.int32)
    return dict(state=state, tangent=tangent, orient=orient, walls=walls)


GAUSS = 0.5773502691896258
XI_SIGNS = (-1.0, -1.0, 1.0, 1.0)
ETA_SIGNS = (-1.0, 1.0, -1.0, 1.0)
MIRRORED_DUOS = ((0, 0), (1, 1), (2, 2), (0, 1), (0, 2), (1, 2))
COLLIDE = 2.0
LOG_TWO_PI = math.log(2.0 * math.pi)


def velocities(slot_index, orient, half_grid):
    spacing = 5.0 / half_grid
    mag_x = ((slot_index // (4 * half_grid)) % half_grid).astype(jnp.float32) + 0.5
    mag_y = ((slot_index // 4) % half_grid).astype(jnp.float32) + 0.5
    level_z = (slot_index // (4 * half_grid * half_grid)).astype(jnp.float32) - (half_grid - 0.5)
    sign_x = (2 * orient[:, 0] - 1).astype(jnp.float32)
    sign_y = (2 * orient[:, 1] - 1).astype(jnp.float32)
    return sign_x * mag_x * spacing, sign_y * mag_y * spacing, level_z * spacing


def moment_table(vel_x, vel_y, molecular_grid_extent, weight):
    return jnp.stack([jnp.ones_like(vel_x), vel_x, vel_y, molecular_grid_extent, vel_x * vel_x, vel_y * vel_y,
                      molecular_grid_extent * molecular_grid_extent, vel_x * vel_y, vel_x * molecular_grid_extent, vel_y * molecular_grid_extent]) * weight


def gauss_points(coef):
    center, grad_x, grad_y = coef[:, 0], coef[:, 1], coef[:, 2]
    return jnp.stack([center + XI_SIGNS[q] * GAUSS * grad_x + ETA_SIGNS[q] * GAUSS * grad_y for q in range(4)], axis=1)


def project_points(values):
    total = values[:, 0] + values[:, 1] + values[:, 2] + values[:, 3]
    along_x = (values[:, 2] + values[:, 3]) - (values[:, 0] + values[:, 1])
    along_y = (values[:, 1] + values[:, 3]) - (values[:, 0] + values[:, 2])
    return jnp.stack([0.25 * total, 0.75 * GAUSS * along_x, 0.75 * GAUSS * along_y], axis=1)


def partner(values):
    dims_in = values.shape
    grouped = values.reshape((dims_in[0] // 4, 2, 2) + dims_in[1:])
    return grouped[:, ::-1].reshape(dims_in)


def full_matrix(entries):
    rows = [[None, None, None], [None, None, None], [None, None, None]]
    for duo_ordinal, (leading_multiplier, trailing_multiplier) in enumerate(MIRRORED_DUOS):
        rows[leading_multiplier][trailing_multiplier] = entries[duo_ordinal]
        rows[trailing_multiplier][leading_multiplier] = entries[duo_ordinal]
    return rows


def gauss_params(moments):
    density = moments[0]
    average_offset = [moments[1 + leading_multiplier] / density for leading_multiplier in range(3)]
    second = [moments[4 + duo_ordinal] for duo_ordinal in range(6)]
    covariance_array = [second[duo_ordinal] / density - average_offset[leading_multiplier] * average_offset[trailing_multiplier] for duo_ordinal, (leading_multiplier, trailing_multiplier) in enumerate(MIRRORED_DUOS)]
    thermal_state = (covariance_array[0] + covariance_array[1] + covariance_array[2]) / 3.0
    pressure_dyad = [(1.5 * thermal_state if leading_multiplier == trailing_multiplier else 0.0) - 0.5 * covariance_array[duo_ordinal] for duo_ordinal, (leading_multiplier, trailing_multiplier) in enumerate(MIRRORED_DUOS)]
    tens_full = full_matrix(pressure_dyad)
    cofactor = [tens_full[1][1] * tens_full[2][2] - tens_full[1][2] * tens_full[1][2],
                tens_full[0][0] * tens_full[2][2] - tens_full[0][2] * tens_full[0][2],
                tens_full[0][0] * tens_full[1][1] - tens_full[0][1] * tens_full[0][1],
                tens_full[0][2] * tens_full[1][2] - tens_full[0][1] * tens_full[2][2],
                tens_full[0][1] * tens_full[1][2] - tens_full[0][2] * tens_full[1][1],
                tens_full[0][1] * tens_full[0][2] - tens_full[0][0] * tens_full[1][2]]
    determinant = tens_full[0][0] * cofactor[0] + tens_full[0][1] * cofactor[3] + tens_full[0][2] * cofactor[4]
    inverse = [entry / determinant for entry in cofactor]
    log_pre = jnp.log(density) - 1.5 * LOG_TWO_PI - 0.5 * jnp.log(determinant)
    delta_density = moments[10]
    drift_delta = [(moments[11 + leading_multiplier] - average_offset[leading_multiplier] * delta_density) / density for leading_multiplier in range(3)]
    dtheta = [moments[14 + duo_ordinal] / density - second[duo_ordinal] * delta_density / (density * density)
              - (drift_delta[leading_multiplier] * average_offset[trailing_multiplier] + average_offset[leading_multiplier] * drift_delta[trailing_multiplier]) for duo_ordinal, (leading_multiplier, trailing_multiplier) in enumerate(MIRRORED_DUOS)]
    temp_delta = (dtheta[0] + dtheta[1] + dtheta[2]) / 3.0
    tens_delta = [(1.5 * temp_delta if leading_multiplier == trailing_multiplier else 0.0) - 0.5 * dtheta[duo_ordinal] for duo_ordinal, (leading_multiplier, trailing_multiplier) in enumerate(MIRRORED_DUOS)]
    inv_full = full_matrix(inverse)
    delta_full = full_matrix(tens_delta)
    trace_term = sum([inv_full[leading_multiplier][trailing_multiplier] * delta_full[trailing_multiplier][leading_multiplier] for leading_multiplier in range(3) for trailing_multiplier in range(3)])
    shift_term = delta_density / density - 0.5 * trace_term
    weight_vec = [inv_full[leading_multiplier][0] * drift_delta[0] + inv_full[leading_multiplier][1] * drift_delta[1] + inv_full[leading_multiplier][2] * drift_delta[2] for leading_multiplier in range(3)]
    inner_prod = [[inv_full[leading_multiplier][0] * delta_full[0][c] + inv_full[leading_multiplier][1] * delta_full[1][c] + inv_full[leading_multiplier][2] * delta_full[2][c]
                   for c in range(3)] for leading_multiplier in range(3)]
    curve_sym = [inner_prod[leading_multiplier][0] * inv_full[0][trailing_multiplier] + inner_prod[leading_multiplier][1] * inv_full[1][trailing_multiplier] + inner_prod[leading_multiplier][2] * inv_full[2][trailing_multiplier]
                 for (leading_multiplier, trailing_multiplier) in MIRRORED_DUOS]
    return jnp.stack(average_offset + inverse + [log_pre, shift_term] + weight_vec + curve_sym)


def quadratic(entries, rel_x, rel_y, rel_z):
    return (entries[0] * rel_x * rel_x + entries[1] * rel_y * rel_y + entries[2] * rel_z * rel_z
            + 2.0 * (entries[3] * rel_x * rel_y + entries[4] * rel_x * rel_z + entries[5] * rel_y * rel_z))


def gauss_tangent(vel_x, vel_y, molecular_grid_extent, params):
    rel_x = vel_x[:, None] - params[0]
    rel_y = vel_y[:, None] - params[1]
    rel_z = molecular_grid_extent[:, None] - params[2]
    gauss = jnp.exp(params[9] - 0.5 * quadratic(params[3:9], rel_x, rel_y, rel_z))
    return gauss * (params[10] + rel_x * params[11] + rel_y * params[12] + rel_z * params[13]
                    + 0.5 * quadratic(params[14:20], rel_x, rel_y, rel_z))


def transport(coef, orient, vel_x, vel_y, left_in, right_in, below_in, above_in):
    center, grad_x, grad_y = coef[:, 0], coef[:, 1], coef[:, 2]
    heads_right = (orient[:, 0] == 1)[:, None, None]
    heads_up = (orient[:, 1] == 1)[:, None, None]
    right_val = jnp.where(heads_right, center + grad_x, right_in[0])
    right_slope = jnp.where(heads_right, grad_y, right_in[1])
    left_val = jnp.where(heads_right, left_in[0], center - grad_x)
    left_slope = jnp.where(heads_right, left_in[1], grad_y)
    top_val = jnp.where(heads_up, center + grad_y, above_in[0])
    top_slope = jnp.where(heads_up, grad_x, above_in[1])
    bottom_val = jnp.where(heads_up, below_in[0], center - grad_y)
    bottom_slope = jnp.where(heads_up, below_in[1], grad_x)
    speed_x = vel_x[:, None, None]
    speed_y = vel_y[:, None, None]
    rate_mean = speed_x * (right_val - left_val) + speed_y * (top_val - bottom_val)
    rate_x = 3.0 * speed_x * (right_val + left_val - 2.0 * center) + speed_y * (top_slope - bottom_slope)
    rate_y = speed_x * (right_slope - left_slope) + 3.0 * speed_y * (top_val + bottom_val - 2.0 * center)
    return jnp.stack([rate_mean, rate_x, rate_y], axis=1)


def reference(state, tangent, orient, walls):
    half_grid = NVX // 2
    weight = (5.0 / half_grid) ** 3
    block_count = 16
    block_size = NV // block_count
    point_count = 4 * CROSSWISE_SLABS * STREAMWISE_SLABS
    slot_all = jnp.arange(NV, dtype=jnp.int32)
    state_blocks = state.reshape(block_count, block_size, 3, CROSSWISE_SLABS, STREAMWISE_SLABS)
    tangent_blocks = tangent.reshape(block_count, block_size, 3, CROSSWISE_SLABS, STREAMWISE_SLABS)
    orient_blocks = orient.reshape(block_count, block_size, 2)
    slot_blocks = slot_all.reshape(block_count, block_size)

    def add_moments(running, pieces):
        state_blk, tangent_blk, orient_blk, slot_blk = pieces
        vel_x, vel_y, molecular_grid_extent = velocities(slot_blk, orient_blk, half_grid)
        moment_rows = moment_table(vel_x, vel_y, molecular_grid_extent, weight)
        part_state = jnp.dot(moment_rows, gauss_points(state_blk).reshape(block_size, point_count),
                             precision=lax.Precision.HIGHEST, preferred_element_type=jnp.float32)
        part_tangent = jnp.dot(moment_rows, gauss_points(tangent_blk).reshape(block_size, point_count),
                               precision=lax.Precision.HIGHEST, preferred_element_type=jnp.float32)
        return running + jnp.concatenate([part_state, part_tangent], axis=0), None

    moments, _ = lax.scan(add_moments, jnp.zeros((20, point_count), jnp.float32),
                          (state_blocks, tangent_blocks, orient_blocks, slot_blocks))
    params = gauss_params(moments)
    floor_flag = walls[0].astype(jnp.float32)
    roof_flag = walls[1].astype(jnp.float32)

    def one_block(pieces):
        tangent_blk, orient_blk, slot_blk = pieces
        vel_x, vel_y, molecular_grid_extent = velocities(slot_blk, orient_blk, half_grid)
        center, grad_x, grad_y = tangent_blk[:, 0], tangent_blk[:, 1], tangent_blk[:, 2]
        left_in = (jnp.roll(center + grad_x, 1, axis=2), jnp.roll(grad_y, 1, axis=2))
        right_in = (jnp.roll(center - grad_x, -1, axis=2), jnp.roll(grad_y, -1, axis=2))
        below_in = (jnp.concatenate([floor_flag * partner(center - grad_y)[:, :1], (center + grad_y)[:, :-1]], axis=1),
                    jnp.concatenate([floor_flag * partner(grad_x)[:, :1], grad_x[:, :-1]], axis=1))
        above_in = (jnp.concatenate([(center - grad_y)[:, 1:], roof_flag * partner(center + grad_y)[:, -1:]], axis=1),
                    jnp.concatenate([grad_x[:, 1:], roof_flag * partner(grad_x)[:, -1:]], axis=1))
        advected = transport(tangent_blk, orient_blk, vel_x, vel_y, left_in, right_in, below_in, above_in)
        gauss_delta = gauss_tangent(vel_x, vel_y, molecular_grid_extent, params).reshape(block_size, 4, CROSSWISE_SLABS, STREAMWISE_SLABS)
        return advected + COLLIDE * (tangent_blk - project_points(gauss_delta))

    result = lax.map(one_block, (tangent_blocks, orient_blocks, slot_blocks))
    return result.reshape(NV, 3, CROSSWISE_SLABS, STREAMWISE_SLABS)
```

```python
import functools
import math

import jax
import jax.numpy as jnp
from jax import lax
from jax.experimental import pallas as pl
from jax.experimental.pallas import tpu as pltpu
from jax.sharding import PartitionSpec as P

MESH = pl.DeviceIdType.MESH
F32 = jnp.float32
BF16 = jnp.bfloat16

SLOTS = 500
PAD = 512
TILES = PAD // 8
HALF = TILES // 2
ROWS = SLOTS * 6
PAD_ROWS = PAD * 6
GAUSS = 0.5773502691896258
LOG_TWO_PI = math.log(2.0 * math.pi)
LOG2E = math.log2(math.e)
DUOS = ((0, 0), (1, 1), (2, 2), (0, 1), (0, 2), (1, 2))
PEERS = 16
ORDER = (8, 7, 9, 6, 10, 5, 11, 4, 12, 3, 13, 2, 14, 1, 15)


def full(entries):
    rows = [[None] * 3 for _ in range(3)]
    for n, (a, b) in enumerate(DUOS):
        rows[a][b] = entries[n]
        rows[b][a] = entries[n]
    return rows


def gauss_coefs(mom):
    rho = mom[0]
    inv_rho = 1.0 / rho
    u = [mom[1 + a] * inv_rho for a in range(3)]
    sec = mom[4:10]
    theta = [sec[n] * inv_rho - u[a] * u[b] for n, (a, b) in enumerate(DUOS)]
    temp = (theta[0] + theta[1] + theta[2]) * (1.0 / 3.0)
    tn = [(1.5 * temp if a == b else 0.0) - 0.5 * theta[n] for n, (a, b) in enumerate(DUOS)]
    t = full(tn)
    cof = [
        t[1][1] * t[2][2] - t[1][2] * t[1][2],
        t[0][0] * t[2][2] - t[0][2] * t[0][2],
        t[0][0] * t[1][1] - t[0][1] * t[0][1],
        t[0][2] * t[1][2] - t[0][1] * t[2][2],
        t[0][1] * t[1][2] - t[0][2] * t[1][1],
        t[0][1] * t[0][2] - t[0][0] * t[1][2],
    ]
    det = t[0][0] * cof[0] + t[0][1] * cof[3] + t[0][2] * cof[4]
    inv_det = 1.0 / det
    inv = [c * inv_det for c in cof]
    log_pre = jnp.log(rho) - 1.5 * LOG_TWO_PI - 0.5 * jnp.log(det)
    drho = mom[10]
    du = [(mom[11 + a] - u[a] * drho) * inv_rho for a in range(3)]
    dlog = drho * inv_rho
    dtheta = [
        (mom[14 + n] - sec[n] * dlog) * inv_rho - (du[a] * u[b] + u[a] * du[b])
        for n, (a, b) in enumerate(DUOS)
    ]
    dtemp = (dtheta[0] + dtheta[1] + dtheta[2]) * (1.0 / 3.0)
    dtn = [(1.5 * dtemp if a == b else 0.0) - 0.5 * dtheta[n] for n, (a, b) in enumerate(DUOS)]
    A = full(inv)
    D = full(dtn)
    trace = sum(A[a][b] * D[b][a] for a in range(3) for b in range(3))
    shift = dlog - 0.5 * trace
    w = [A[a][0] * du[0] + A[a][1] * du[1] + A[a][2] * du[2] for a in range(3)]
    AD = [[A[a][0] * D[0][c] + A[a][1] * D[1][c] + A[a][2] * D[2][c] for c in range(3)] for a in range(3)]
    curve = [AD[a][0] * A[0][b] + AD[a][1] * A[1][b] + AD[a][2] * A[2][b] for a, b in DUOS]
    B = full(curve)
    au = [A[a][0] * u[0] + A[a][1] * u[1] + A[a][2] * u[2] for a in range(3)]
    bu = [B[a][0] * u[0] + B[a][1] * u[1] + B[a][2] * u[2] for a in range(3)]
    e0 = log_pre - 0.5 * (u[0] * au[0] + u[1] * au[1] + u[2] * au[2])
    expo = [e0] + au + [-0.5 * inv[n] if n < 3 else -inv[n] for n in range(6)]
    q0 = shift - (u[0] * w[0] + u[1] * w[1] + u[2] * w[2]) + 0.5 * (u[0] * bu[0] + u[1] * bu[1] + u[2] * bu[2])
    fact = [q0] + [w[a] - bu[a] for a in range(3)] + [0.5 * curve[n] if n < 3 else curve[n] for n in range(6)]
    return [x * LOG2E for x in expo], [x * -0.5 for x in fact]


def split3(x):
    hi = x.astype(BF16).astype(F32)
    r = x - hi
    mid = r.astype(BF16).astype(F32)
    return hi, mid, r - mid


def mirror(x, low_pair):
    return jnp.where(low_pair, pltpu.roll(x, 6, 0), pltpu.roll(x, 2, 0))


def kernel(
    state_hbm, tan_hbm, orient_hbm, walls_hbm, out_hbm,
    xs, xt, ob, tb, orient_v, bits, walls_v, mg, ml, vxy, xsp, part, rx1, sumt, tot,
    vsend, vrecv, xsend, xleft, xright, cs, csb, eq,
    lsem, s1, r1, s2, r2, ysem, xsem_s, xsem_r, osem,
):
    me = lax.axis_index("vert")
    gx = lax.axis_index("gx")
    gy = lax.axis_index("gy")
    wall = gy
    inner = 1 - gy
    load_t = pltpu.make_async_copy(tan_hbm, xt.at[pl.ds(0, ROWS)], lsem.at[0])
    load_s = pltpu.make_async_copy(state_hbm, xs.at[pl.ds(0, ROWS)], lsem.at[1])
    load_o = pltpu.make_async_copy(orient_hbm, orient_v, lsem.at[2])
    load_w = pltpu.make_async_copy(walls_hbm, walls_v, lsem.at[3])
    load_o.start()
    load_t.start()
    load_s.start()
    load_w.start()

    barrier = pltpu.get_barrier_semaphore()
    for d in ORDER:
        pl.semaphore_signal(barrier, inc=1, device_id={"vert": lax.rem(me + d, PEERS)}, device_id_type=MESH)
    pl.semaphore_signal(barrier, inc=1, device_id={"gy": inner}, device_id_type=MESH)
    east = lax.rem(gx + 1, 8)
    west = lax.rem(gx + 7, 8)
    pl.semaphore_signal(barrier, inc=1, device_id={"gx": east}, device_id_type=MESH)
    pl.semaphore_signal(barrier, inc=1, device_id={"gx": west}, device_id_type=MESH)

    zeros_tail = jnp.zeros((PAD_ROWS - ROWS, 128), F32)
    xs[pl.ds(ROWS, PAD_ROWS - ROWS), :] = zeros_tail
    xt[pl.ds(ROWS, PAD_ROWS - ROWS), :] = zeros_tail
    bits[...] = jnp.zeros((2, PAD), F32)
    load_o.wait()
    bits[:, 0:SLOTS] = orient_v[...].astype(F32)
    row = lax.broadcasted_iota(jnp.int32, (8, PAD), 0)
    slot = (lax.broadcasted_iota(jnp.int32, (8, PAD), 1) + me * SLOTS).astype(F32) + 0.5
    by40 = jnp.floor(slot * (1.0 / 40.0))
    by400 = jnp.floor(slot * (1.0 / 400.0))
    by4 = jnp.floor(slot * 0.25)
    sx = jnp.broadcast_to(bits[0:1, :], (8, PAD)) * 2.0 - 1.0
    sy = jnp.broadcast_to(bits[1:2, :], (8, PAD)) * 2.0 - 1.0
    vx = sx * (by40 - 10.0 * by400 + 0.5) * 0.5
    vy = sy * (by4 - 10.0 * by40 + 0.5) * 0.5
    vz = (by400 - 9.5) * 0.5
    quad = [vx * vx, vy * vy, vz * vz, vx * vy, vx * vz, vy * vz]
    qhi = [q.astype(BF16).astype(F32) for q in quad]
    qlo = [q - h for q, h in zip(quad, qhi)]
    lin = [jnp.ones((8, PAD), F32), vx, vy, vz]
    zero = jnp.zeros((8, PAD), F32)

    def pick(values):
        out = values[0]
        for k in range(1, 8):
            out = jnp.where(row == k, values[k], out)
        return out

    head = pick(lin + qhi[:4])
    tail = pick(qhi[4:] + qlo)
    lows = pick([zero] * 4 + qlo[:4])
    even = lax.rem(row, 2) == 0
    pair_hi = jnp.where(even, qhi[4], qhi[5])
    pair_lo = jnp.where(even, qlo[4], qlo[5])
    ml[...] = (jnp.concatenate([head, lows, pair_hi, pair_lo], axis=0) * 0.125).astype(BF16)
    table = jnp.concatenate([head, tail] * 3 + [zero] * 10, axis=0)
    mg[...] = jnp.transpose(table).astype(BF16)
    krow = lax.broadcasted_iota(jnp.int32, (128, 256), 0)
    kcol = lax.broadcasted_iota(jnp.int32, (128, 256), 1)
    choose = jnp.where(krow == 1 + (kcol >> 7), 1.0, 0.0).astype(BF16)
    vxy[...] = jnp.dot(mg[...], choose, preferred_element_type=F32)
    csb[...] = jnp.zeros(csb.shape, BF16)

    sub = lax.broadcasted_iota(jnp.int32, (8, 128), 0)
    lane = lax.broadcasted_iota(jnp.int32, (8, 128), 1)
    low_pair = lax.rem(sub, 4) < 2
    toward = (1 - 2 * gy).astype(F32)

    def comp(tile, coef, y):
        return xt[pl.ds(tile * 48 + coef * 2 + y, 8, stride=6), :]

    def speed_x(tile):
        return vxy[pl.ds(pl.multiple_of(tile * 8, 8), 8), 0:128]

    def speed_y(tile):
        return vxy[pl.ds(pl.multiple_of(tile * 8, 8), 8), 128:256]

    load_t.wait()

    def pack_rows(t, carry):
        traces = []
        for tile in (t, t + HALF):
            v = speed_y(tile)
            sgn = jnp.where(v > 0.0, 1.0, -1.0)
            value = comp(tile, 0, inner) + sgn * comp(tile, 2, inner)
            traces.append((v * toward > 0.0, value, comp(tile, 1, inner)))
        (in0, val0, slo0), (in1, val1, slo1) = traces
        base = pl.multiple_of(t * 16, 16)
        vsend[pl.ds(base, 8), :] = jnp.where(in0, val0, jnp.where(in1, val1, mirror(val1, low_pair)))
        vsend[pl.ds(base + 8, 8), :] = jnp.where(in0, slo0, jnp.where(in1, slo1, mirror(slo1, low_pair)))
        return carry

    lax.fori_loop(0, HALF, pack_rows, 0, unroll=2)
    pl.semaphore_wait(barrier, PEERS + 2)
    send_y = pltpu.make_async_remote_copy(
        src_ref=vsend, dst_ref=vrecv, send_sem=ysem.at[0], recv_sem=ysem.at[1],
        device_id={"gy": inner}, device_id_type=MESH,
    )
    send_y.start()

    def spread(ref, first):
        def body(t, carry):
            for j in range(6):
                hi, mid, lo = split3(ref[pl.ds(t * 96 + j, 16, stride=6), :])
                rows16 = pl.ds(pl.multiple_of(t * 16, 16), 16)
                cols = pl.ds((j % 2) * 128, 128)
                xsp[first + j // 2, 0, rows16, cols] = hi.astype(BF16)
                xsp[first + j // 2, 1, rows16, cols] = mid.astype(BF16)
                xsp[first + j // 2, 2, rows16, cols] = lo.astype(BF16)
            return carry

        lax.fori_loop(0, PAD // 16, body, 0)

    spread(xt, 3)
    load_s.wait()
    spread(xs, 0)
    group = sub // 2
    packed = [None] * 3
    for p in range(6):
        acc = jnp.dot(ml[...], xsp[p, 0], preferred_element_type=F32)
        acc += jnp.dot(ml[...], xsp[p, 1], preferred_element_type=F32)
        acc += jnp.dot(ml[...], xsp[p, 2], preferred_element_type=F32)
        for h in range(2):
            c = 2 * p + h
            cols = slice(h * 128, h * 128 + 128)
            part[pl.ds(c * 8, 8), :] = acc[0:8, cols] + acc[8:16, cols]
            extra = acc[16:24, cols] + acc[24:32, cols]
            old = packed[c // 4]
            packed[c // 4] = extra if old is None else jnp.where(group == c % 4, extra, old)
    for i in range(3):
        part[pl.ds((12 + i) * 8, 8), :] = packed[i]
    part[pl.ds(120, 8), :] = jnp.zeros((8, 128), F32)

    first = []
    for d in ORDER:
        peer = lax.rem(me + d, PEERS)
        copy = pltpu.make_async_remote_copy(
            src_ref=part.at[pl.ds(pl.multiple_of(peer * 8, 8), 8)],
            dst_ref=rx1.at[pl.ds((15 - d) * 8, 8)],
            send_sem=s1.at[d - 1], recv_sem=r1.at[d - 1],
            device_id={"vert": peer}, device_id_type=MESH,
        )
        copy.start()
        first.append(copy)

    def pack_cols(t, carry):
        acc0, acc1, signs = carry
        v = speed_x(t)
        right = v > 0.0
        sgn = jnp.where(right, 1.0, -1.0)
        for y in range(2):
            value = comp(t, 0, y) + sgn * comp(t, 1, y)
            slope = comp(t, 2, y)
            at = y * 64 + t
            here = lane == at
            edge0 = jnp.where(right, pltpu.roll(value, 1, 1), value)
            edge1 = jnp.where(right, pltpu.roll(slope, 1, 1), slope)
            acc0 = jnp.where(here, pltpu.roll(edge0, at, 1), acc0)
            acc1 = jnp.where(here, pltpu.roll(edge1, at, 1), acc1)
            signs = jnp.where(here, sgn, signs)
        return acc0, acc1, signs

    blank = jnp.zeros((8, 128), F32)
    acc0, acc1, signs = lax.fori_loop(0, TILES, pack_cols, (blank, blank, blank))
    xsend[0:8, :] = acc0
    xsend[8:16, :] = acc1
    send_e = pltpu.make_async_remote_copy(
        src_ref=xsend, dst_ref=xleft, send_sem=xsem_s.at[0], recv_sem=xsem_r.at[0],
        device_id={"gx": east}, device_id_type=MESH,
    )
    send_w = pltpu.make_async_remote_copy(
        src_ref=xsend, dst_ref=xright, send_sem=xsem_s.at[1], recv_sem=xsem_r.at[1],
        device_id={"gx": west}, device_id_type=MESH,
    )
    send_e.start()
    send_w.start()

    for copy in first:
        copy.wait_recv()
    mine = pl.ds(pl.multiple_of(me * 8, 8), 8)
    total = part[mine, :]
    for k in range(15):
        total = total + rx1[pl.ds(k * 8, 8), :]
    sumt[...] = total
    tot[mine, :] = total
    second = []
    for d in ORDER:
        copy = pltpu.make_async_remote_copy(
            src_ref=sumt, dst_ref=tot.at[mine],
            send_sem=s2.at[d - 1], recv_sem=r2.at[d - 1],
            device_id={"vert": lax.rem(me + d, PEERS)}, device_id_type=MESH,
        )
        copy.start()
        second.append(copy)

    send_e.wait_recv()
    send_w.wait_recv()
    from_left = signs > 0.0
    edge_val = jnp.where(from_left, xleft[0:8, :], xright[0:8, :])
    edge_slo = jnp.where(from_left, xleft[8:16, :], xright[8:16, :])
    send_y.wait_recv()
    load_w.wait()
    flags = walls_v[pl.ds(wall, 1), :].astype(F32)
    flag = jnp.broadcast_to(flags, (8, 128))

    def move(t, carry):
        base = pl.multiple_of(t * 16, 16)
        far = [vrecv[pl.ds(base, 8), :], vrecv[pl.ds(base + 8, 8), :]]
        first_in = None
        for n, tile in enumerate((t, t + HALF)):
            v_x = speed_x(tile)
            v_y = speed_y(tile)
            right = v_x > 0.0
            s_x = jnp.where(right, 1.0, -1.0)
            s_y = jnp.where(v_y > 0.0, 1.0, -1.0)
            a_x = jnp.abs(v_x)
            a_y = jnp.abs(v_y)
            inward = v_y * toward > 0.0
            if n == 0:
                first_in = inward
                halo = far
            else:
                halo = [jnp.where(first_in, f, mirror(f, low_pair)) for f in far]
            cw, gxw, gyw = (comp(tile, k, wall) for k in range(3))
            ci, gxi, gyi = (comp(tile, k, inner) for k in range(3))
            fw = cw + s_y * gyw
            fi = ci + s_y * gyi
            u_w = (
                jnp.where(inward, flag * mirror(fw, low_pair), fi),
                jnp.where(inward, flag * mirror(gxw, low_pair), gxi),
            )
            u_i = (jnp.where(inward, fw, halo[0]), jnp.where(inward, gxw, halo[1]))
            outermost = lane == jnp.where(right, 0, 127)
            for y, c, g_x, g_y, f_y, (uy0, uy1) in (
                (wall, cw, gxw, gyw, fw, u_w),
                (inner, ci, gxi, gyi, fi, u_i),
            ):
                f_x = c + s_x * g_x
                back = lax.rem(256 - (y * 64 + tile), 128)
                e0 = pltpu.roll(edge_val, back, 1)
                e1 = pltpu.roll(edge_slo, back, 1)
                e0 = jnp.where(right, e0, pltpu.roll(e0, 127, 1))
                e1 = jnp.where(right, e1, pltpu.roll(e1, 127, 1))
                ux0 = jnp.where(right, pltpu.roll(f_x, 1, 1), pltpu.roll(f_x, 127, 1))
                ux2 = jnp.where(right, pltpu.roll(g_y, 1, 1), pltpu.roll(g_y, 127, 1))
                ux0 = jnp.where(outermost, e0, ux0)
                ux2 = jnp.where(outermost, e1, ux2)
                c2 = c + c
                mean = a_x * (f_x - ux0) + a_y * (f_y - uy0) + c2
                rx = 3.0 * v_x * (f_x + ux0 - c2) + a_y * (g_x - uy1) + 2.0 * g_x
                ry = a_x * (g_y - ux2) + 3.0 * v_y * (f_y + uy0 - c2) + 2.0 * g_y
                for k, value in enumerate((mean, rx, ry)):
                    at = pl.multiple_of((tile * 6 + k * 2 + y) * 8, 8)
                    tb[pl.ds(at, 8), :] = value
        return carry

    lax.fori_loop(0, HALF, move, 0)

    for copy in second:
        copy.wait_recv()
    upper = sub >= 4
    q_of = lax.rem(sub, 4)
    xi = jnp.where(q_of >= 2, GAUSS, -GAUSS)
    eta = jnp.where(lax.rem(q_of, 2) == 1, GAUSS, -GAUSS)

    def moment(k):
        s, n = divmod(k, 10)
        coefs = []
        for j in range(6):
            c = s * 6 + j
            at = c * 8 + n if n < 8 else (12 + c // 4) * 8 + (c % 4) * 2 + n - 8
            coefs.append(jnp.broadcast_to(tot[pl.ds(at, 1), :], (8, 128)))
        a, b, c = (jnp.where(upper, coefs[2 * m + 1], coefs[2 * m]) for m in range(3))
        return a + xi * b + eta * c

    expo, fact = gauss_coefs([moment(k) for k in range(20)])
    for half, coefs in enumerate((expo, fact)):
        for k, x in enumerate(coefs):
            for n, piece in enumerate(split3(x)):
                for r in (k,) if k < 4 else (k, k + 6):
                    cs[pl.ds(half * 384 + n * 16 + r, 8, stride=48), :] = piece
    for i in range(8):
        csb[i, 0:48, 0:128] = cs[i * 48 : i * 48 + 48, :].astype(BF16)
        csb[i, 0:48, 128:256] = cs[384 + i * 48 : 384 + i * 48 + 48, :].astype(BF16)
    for i in range(8):
        eq[i] = jnp.dot(mg[...], csb[i], preferred_element_type=F32)

    stores = []
    quarter = TILES // 4
    for part_no in range(4):
        def finish(t, carry):
            rows8 = pl.ds(pl.multiple_of(t * 8, 8), 8)
            for y in range(2):
                g = [jnp.exp2(eq[y * 4 + q, rows8, 0:128]) * eq[y * 4 + q, rows8, 128:256] for q in range(4)]
                low = g[0] + g[1]
                high = g[2] + g[3]
                vals = (
                    low + high,
                    (3.0 * GAUSS) * (high - low),
                    (3.0 * GAUSS) * ((g[1] - g[0]) + (g[3] - g[2])),
                )
                for k in range(3):
                    at = pl.multiple_of((t * 6 + k * 2 + y) * 8, 8)
                    ob[pl.ds(t * 48 + k * 2 + y, 8, stride=6), :] = tb[pl.ds(at, 8), :] + vals[k]
            return carry

        lax.fori_loop(part_no * quarter, (part_no + 1) * quarter, finish, 0, unroll=2)
        begin = part_no * quarter * 48
        size = min(quarter * 48, ROWS - begin)
        store = pltpu.make_async_copy(ob.at[pl.ds(begin, size)], out_hbm.at[pl.ds(begin, size)], osem.at[part_no])
        store.start()
        stores.append(store)

    for copy in first + second + [send_y, send_e, send_w]:
        copy.wait_send()
    for store in stores:
        store.wait()


def shards(state, tangent, orient, walls):
    hbm = pl.BlockSpec(memory_space=pltpu.HBM)
    out = pl.pallas_call(
        kernel,
        out_shape=jax.ShapeDtypeStruct((ROWS, 128), F32),
        in_specs=[hbm] * 4,
        out_specs=hbm,
        scratch_shapes=[
            pltpu.VMEM((PAD_ROWS, 128), F32),
            pltpu.VMEM((PAD_ROWS, 128), F32),
            pltpu.VMEM((PAD_ROWS, 128), F32),
            pltpu.VMEM((PAD_ROWS, 128), F32),
            pltpu.VMEM((2, SLOTS), jnp.int32),
            pltpu.VMEM((2, PAD), F32),
            pltpu.VMEM((2, 128), jnp.int32),
            pltpu.VMEM((PAD, 128), BF16),
            pltpu.VMEM((32, PAD), BF16),
            pltpu.VMEM((PAD, 256), F32),
            pltpu.VMEM((6, 3, PAD, 256), BF16),
            pltpu.VMEM((128, 128), F32),
            pltpu.VMEM((120, 128), F32),
            pltpu.VMEM((8, 128), F32),
            pltpu.VMEM((128, 128), F32),
            pltpu.VMEM((HALF * 16, 128), F32),
            pltpu.VMEM((HALF * 16, 128), F32),
            pltpu.VMEM((16, 128), F32),
            pltpu.VMEM((16, 128), F32),
            pltpu.VMEM((16, 128), F32),
            pltpu.VMEM((16 * 48, 128), F32),
            pltpu.VMEM((8, 128, 256), BF16),
            pltpu.VMEM((8, PAD, 256), F32),
            pltpu.SemaphoreType.DMA((4,)),
            pltpu.SemaphoreType.DMA((15,)),
            pltpu.SemaphoreType.DMA((15,)),
            pltpu.SemaphoreType.DMA((15,)),
            pltpu.SemaphoreType.DMA((15,)),
            pltpu.SemaphoreType.DMA((2,)),
            pltpu.SemaphoreType.DMA((2,)),
            pltpu.SemaphoreType.DMA((2,)),
            pltpu.SemaphoreType.DMA((4,)),
        ],
        compiler_params=pltpu.CompilerParams(
            collective_id=0, has_side_effects=True, vmem_limit_bytes=60 * 1024 * 1024
        ),
    )(
        state.reshape(ROWS, 128),
        tangent.reshape(ROWS, 128),
        orient.T,
        walls,
    )
    return out.reshape(SLOTS, 3, 2, 128)


def solution(mesh):
    placed = (
        P("vert", None, "gy", "gx"),
        P("vert", None, "gy", "gx"),
        P("vert", None),
        P(None, "gx"),
    )
    return jax.shard_map(
        shards, mesh=mesh, in_specs=placed, out_specs=P("vert", None, "gy", "gx"), check_vma=False
    )
```

```python
import functools
import math

import jax
import jax.numpy as jnp
from jax import lax
from jax.experimental import pallas as pl
from jax.experimental.pallas import tpu as pltpu
from jax.sharding import PartitionSpec as P

MESH = pl.DeviceIdType.MESH
F32 = jnp.float32
BF16 = jnp.bfloat16

SLOTS = 500
PAD = 512
TILES = PAD // 8
HALF = TILES // 2
ROWS = SLOTS * 6
PAD_ROWS = PAD * 6
GAUSS = 0.5773502691896258
LOG_TWO_PI = math.log(2.0 * math.pi)
LOG2E = math.log2(math.e)
DUOS = ((0, 0), (1, 1), (2, 2), (0, 1), (0, 2), (1, 2))
PEERS = 16
ORDER = (8, 7, 9, 6, 10, 5, 11, 4, 12, 3, 13, 2, 14, 1, 15)


def full(entries):
    rows = [[None] * 3 for _ in range(3)]
    for n, (a, b) in enumerate(DUOS):
        rows[a][b] = entries[n]
        rows[b][a] = entries[n]
    return rows


def gauss_coefs(mom):
    rho = mom[0]
    inv_rho = 1.0 / rho
    u = [mom[1 + a] * inv_rho for a in range(3)]
    sec = mom[4:10]
    theta = [sec[n] * inv_rho - u[a] * u[b] for n, (a, b) in enumerate(DUOS)]
    temp = (theta[0] + theta[1] + theta[2]) * (1.0 / 3.0)
    tn = [(1.5 * temp if a == b else 0.0) - 0.5 * theta[n] for n, (a, b) in enumerate(DUOS)]
    t = full(tn)
    cof = [
        t[1][1] * t[2][2] - t[1][2] * t[1][2],
        t[0][0] * t[2][2] - t[0][2] * t[0][2],
        t[0][0] * t[1][1] - t[0][1] * t[0][1],
        t[0][2] * t[1][2] - t[0][1] * t[2][2],
        t[0][1] * t[1][2] - t[0][2] * t[1][1],
        t[0][1] * t[0][2] - t[0][0] * t[1][2],
    ]
    det = t[0][0] * cof[0] + t[0][1] * cof[3] + t[0][2] * cof[4]
    inv_det = 1.0 / det
    inv = [c * inv_det for c in cof]
    log_pre = jnp.log(rho) - 1.5 * LOG_TWO_PI - 0.5 * jnp.log(det)
    drho = mom[10]
    du = [(mom[11 + a] - u[a] * drho) * inv_rho for a in range(3)]
    dlog = drho * inv_rho
    dtheta = [
        (mom[14 + n] - sec[n] * dlog) * inv_rho - (du[a] * u[b] + u[a] * du[b])
        for n, (a, b) in enumerate(DUOS)
    ]
    dtemp = (dtheta[0] + dtheta[1] + dtheta[2]) * (1.0 / 3.0)
    dtn = [(1.5 * dtemp if a == b else 0.0) - 0.5 * dtheta[n] for n, (a, b) in enumerate(DUOS)]
    A = full(inv)
    D = full(dtn)
    trace = sum(A[a][b] * D[b][a] for a in range(3) for b in range(3))
    shift = dlog - 0.5 * trace
    w = [A[a][0] * du[0] + A[a][1] * du[1] + A[a][2] * du[2] for a in range(3)]
    AD = [[A[a][0] * D[0][c] + A[a][1] * D[1][c] + A[a][2] * D[2][c] for c in range(3)] for a in range(3)]
    curve = [AD[a][0] * A[0][b] + AD[a][1] * A[1][b] + AD[a][2] * A[2][b] for a, b in DUOS]
    B = full(curve)
    au = [A[a][0] * u[0] + A[a][1] * u[1] + A[a][2] * u[2] for a in range(3)]
    bu = [B[a][0] * u[0] + B[a][1] * u[1] + B[a][2] * u[2] for a in range(3)]
    e0 = log_pre - 0.5 * (u[0] * au[0] + u[1] * au[1] + u[2] * au[2])
    expo = [e0] + au + [-0.5 * inv[n] if n < 3 else -inv[n] for n in range(6)]
    q0 = shift - (u[0] * w[0] + u[1] * w[1] + u[2] * w[2]) + 0.5 * (u[0] * bu[0] + u[1] * bu[1] + u[2] * bu[2])
    fact = [q0] + [w[a] - bu[a] for a in range(3)] + [0.5 * curve[n] if n < 3 else curve[n] for n in range(6)]
    return [x * LOG2E for x in expo], [x * -0.5 for x in fact]


def split3(x):
    hi = x.astype(BF16).astype(F32)
    r = x - hi
    mid = r.astype(BF16).astype(F32)
    return hi, mid, r - mid


def mirror(x, low_pair):
    return jnp.where(low_pair, pltpu.roll(x, 6, 0), pltpu.roll(x, 2, 0))


def gather(
    state_hbm, tan_hbm, orient_hbm, walls_hbm, tb, mg, csb,
    xs, xt, orient_v, bits, walls_v, ml, vxy, xsp, part, rx1, sumt, tot,
    vsend, vrecv, xsend, xleft, xright, edges, cs,
    lsem, s1, r1, s2, r2, ysem, xsem_s, xsem_r,
):
    me = lax.axis_index("vert")
    gx = lax.axis_index("gx")
    gy = lax.axis_index("gy")
    wall = gy
    inner = 1 - gy
    load_t = pltpu.make_async_copy(tan_hbm, xt.at[pl.ds(0, ROWS)], lsem.at[0])
    load_s = pltpu.make_async_copy(state_hbm, xs.at[pl.ds(0, ROWS)], lsem.at[1])
    load_o = pltpu.make_async_copy(orient_hbm, orient_v, lsem.at[2])
    load_w = pltpu.make_async_copy(walls_hbm, walls_v, lsem.at[3])
    load_o.start()
    load_t.start()
    load_s.start()
    load_w.start()

    barrier = pltpu.get_barrier_semaphore()
    for d in ORDER:
        pl.semaphore_signal(barrier, inc=1, device_id={"vert": lax.rem(me + d, PEERS)}, device_id_type=MESH)
    pl.semaphore_signal(barrier, inc=1, device_id={"gy": inner}, device_id_type=MESH)
    east = lax.rem(gx + 1, 8)
    west = lax.rem(gx + 7, 8)
    pl.semaphore_signal(barrier, inc=1, device_id={"gx": east}, device_id_type=MESH)
    pl.semaphore_signal(barrier, inc=1, device_id={"gx": west}, device_id_type=MESH)

    zeros_tail = jnp.zeros((PAD_ROWS - ROWS, 128), F32)
    xs[pl.ds(ROWS, PAD_ROWS - ROWS), :] = zeros_tail
    xt[pl.ds(ROWS, PAD_ROWS - ROWS), :] = zeros_tail
    bits[...] = jnp.zeros((2, PAD), F32)
    load_o.wait()
    bits[:, 0:SLOTS] = orient_v[...].astype(F32)
    row = lax.broadcasted_iota(jnp.int32, (8, PAD), 0)
    slot = (lax.broadcasted_iota(jnp.int32, (8, PAD), 1) + me * SLOTS).astype(F32) + 0.5
    by40 = jnp.floor(slot * (1.0 / 40.0))
    by400 = jnp.floor(slot * (1.0 / 400.0))
    by4 = jnp.floor(slot * 0.25)
    sx = jnp.broadcast_to(bits[0:1, :], (8, PAD)) * 2.0 - 1.0
    sy = jnp.broadcast_to(bits[1:2, :], (8, PAD)) * 2.0 - 1.0
    vx = sx * (by40 - 10.0 * by400 + 0.5) * 0.5
    vy = sy * (by4 - 10.0 * by40 + 0.5) * 0.5
    vz = (by400 - 9.5) * 0.5
    quad = [vx * vx, vy * vy, vz * vz, vx * vy, vx * vz, vy * vz]
    qhi = [q.astype(BF16).astype(F32) for q in quad]
    qlo = [q - h for q, h in zip(quad, qhi)]
    lin = [jnp.ones((8, PAD), F32), vx, vy, vz]
    zero = jnp.zeros((8, PAD), F32)

    def pick(values):
        out = values[0]
        for k in range(1, 8):
            out = jnp.where(row == k, values[k], out)
        return out

    head = pick(lin + qhi[:4])
    tail = pick(qhi[4:] + qlo)
    lows = pick([zero] * 4 + qlo[:4])
    even = lax.rem(row, 2) == 0
    pair_hi = jnp.where(even, qhi[4], qhi[5])
    pair_lo = jnp.where(even, qlo[4], qlo[5])
    ml[...] = (jnp.concatenate([head, lows, pair_hi, pair_lo], axis=0) * 0.125).astype(BF16)
    table = jnp.concatenate([head, tail] * 3 + [zero] * 10, axis=0)
    mg[...] = jnp.transpose(table).astype(BF16)
    krow = lax.broadcasted_iota(jnp.int32, (128, 256), 0)
    kcol = lax.broadcasted_iota(jnp.int32, (128, 256), 1)
    choose = jnp.where(krow == 1 + (kcol >> 7), 1.0, 0.0).astype(BF16)
    vxy[...] = jnp.dot(mg[...], choose, preferred_element_type=F32)
    csb[...] = jnp.zeros(csb.shape, BF16)

    sub = lax.broadcasted_iota(jnp.int32, (8, 128), 0)
    lane = lax.broadcasted_iota(jnp.int32, (8, 128), 1)
    low_pair = lax.rem(sub, 4) < 2
    toward = (1 - 2 * gy).astype(F32)

    def comp(tile, coef, y):
        return xt[pl.ds(tile * 48 + coef * 2 + y, 8, stride=6), :]

    def speed_x(tile):
        return vxy[pl.ds(pl.multiple_of(tile * 8, 8), 8), 0:128]

    def speed_y(tile):
        return vxy[pl.ds(pl.multiple_of(tile * 8, 8), 8), 128:256]

    load_t.wait()

    def pack_rows(t, carry):
        traces = []
        for tile in (t, t + HALF):
            v = speed_y(tile)
            sgn = jnp.where(v > 0.0, 1.0, -1.0)
            value = comp(tile, 0, inner) + sgn * comp(tile, 2, inner)
            traces.append((v * toward > 0.0, value, comp(tile, 1, inner)))
        (in0, val0, slo0), (in1, val1, slo1) = traces
        base = pl.multiple_of(t * 16, 16)
        vsend[pl.ds(base, 8), :] = jnp.where(in0, val0, jnp.where(in1, val1, mirror(val1, low_pair)))
        vsend[pl.ds(base + 8, 8), :] = jnp.where(in0, slo0, jnp.where(in1, slo1, mirror(slo1, low_pair)))
        return carry

    lax.fori_loop(0, HALF, pack_rows, 0, unroll=4)

    def spread(ref, first):
        def body(t, carry):
            for j in range(6):
                hi, mid, lo = split3(ref[pl.ds(t * 96 + j, 16, stride=6), :])
                rows16 = pl.ds(pl.multiple_of(t * 16, 16), 16)
                cols = pl.ds((j % 2) * 128, 128)
                xsp[first + j // 2, 0, rows16, cols] = hi.astype(BF16)
                xsp[first + j // 2, 1, rows16, cols] = mid.astype(BF16)
                xsp[first + j // 2, 2, rows16, cols] = lo.astype(BF16)
            return carry

        lax.fori_loop(0, PAD // 16, body, 0)

    spread(xt, 3)
    pl.semaphore_wait(barrier, PEERS + 2)
    send_y = pltpu.make_async_remote_copy(
        src_ref=vsend, dst_ref=vrecv, send_sem=ysem.at[0], recv_sem=ysem.at[1],
        device_id={"gy": inner}, device_id_type=MESH,
    )
    send_y.start()
    load_s.wait()
    spread(xs, 0)
    group = sub // 2
    packed = [None] * 3
    for p in range(6):
        acc = jnp.dot(ml[...], xsp[p, 0], preferred_element_type=F32)
        acc += jnp.dot(ml[...], xsp[p, 1], preferred_element_type=F32)
        acc += jnp.dot(ml[...], xsp[p, 2], preferred_element_type=F32)
        for h in range(2):
            c = 2 * p + h
            cols = slice(h * 128, h * 128 + 128)
            part[pl.ds(c * 8, 8), :] = acc[0:8, cols] + acc[8:16, cols]
            extra = acc[16:24, cols] + acc[24:32, cols]
            old = packed[c // 4]
            packed[c // 4] = extra if old is None else jnp.where(group == c % 4, extra, old)
    for i in range(3):
        part[pl.ds((12 + i) * 8, 8), :] = packed[i]
    part[pl.ds(120, 8), :] = jnp.zeros((8, 128), F32)

    first = []
    for d in ORDER:
        peer = lax.rem(me + d, PEERS)
        copy = pltpu.make_async_remote_copy(
            src_ref=part.at[pl.ds(pl.multiple_of(peer * 8, 8), 8)],
            dst_ref=rx1.at[pl.ds((15 - d) * 8, 8)],
            send_sem=s1.at[d - 1], recv_sem=r1.at[d - 1],
            device_id={"vert": peer}, device_id_type=MESH,
        )
        copy.start()
        first.append(copy)

    def pack_cols(v, carry):
        acc = jnp.zeros((8, 128), F32)
        for n in range(HALF):
            tile = v * HALF + n
            right = speed_x(tile) > 0.0
            sgn = jnp.where(right, 1.0, -1.0)
            for y in range(2):
                value = comp(tile, 0, y) + sgn * comp(tile, 1, y)
                for k, x in enumerate((value, comp(tile, 2, y))):
                    at = n * 4 + y * 2 + k
                    moved = jnp.where(right, pltpu.roll(x, (at + 1) % 128, 1), pltpu.roll(x, at, 1) if at else x)
                    acc = jnp.where(lane == at, moved, acc)
        xsend[pl.ds(pl.multiple_of(v * 8, 8), 8), :] = acc
        return carry

    lax.fori_loop(0, 2, pack_cols, 0)
    send_e = pltpu.make_async_remote_copy(
        src_ref=xsend, dst_ref=xleft, send_sem=xsem_s.at[0], recv_sem=xsem_r.at[0],
        device_id={"gx": east}, device_id_type=MESH,
    )
    send_w = pltpu.make_async_remote_copy(
        src_ref=xsend, dst_ref=xright, send_sem=xsem_s.at[1], recv_sem=xsem_r.at[1],
        device_id={"gx": west}, device_id_type=MESH,
    )
    send_e.start()
    send_w.start()

    for copy in first:
        copy.wait_recv()
    mine = pl.ds(pl.multiple_of(me * 8, 8), 8)
    total = part[mine, :]
    for k in range(15):
        total = total + rx1[pl.ds(k * 8, 8), :]
    sumt[...] = total
    tot[mine, :] = total
    second = []
    for d in ORDER:
        copy = pltpu.make_async_remote_copy(
            src_ref=sumt, dst_ref=tot.at[mine],
            send_sem=s2.at[d - 1], recv_sem=r2.at[d - 1],
            device_id={"vert": lax.rem(me + d, PEERS)}, device_id_type=MESH,
        )
        copy.start()
        second.append(copy)

    send_e.wait_recv()
    send_w.wait_recv()

    def unpack_cols(v, carry):
        rows8 = pl.ds(pl.multiple_of(v * 8, 8), 8)
        west_in = xleft[rows8, :]
        east_in = xright[rows8, :]
        for n in range(HALF):
            tile = v * HALF + n
            right = speed_x(tile) > 0.0
            for k in range(4):
                at = slice(n * 4 + k, n * 4 + k + 1)
                value = jnp.where(right, jnp.broadcast_to(west_in[:, at], (8, 128)), jnp.broadcast_to(east_in[:, at], (8, 128)))
                edges[pl.ds(pl.multiple_of((tile * 4 + k) * 8, 8), 8), :] = value
        return carry

    lax.fori_loop(0, 2, unpack_cols, 0)
    send_y.wait_recv()
    load_w.wait()
    flags = walls_v[pl.ds(wall, 1), :].astype(F32)
    flag = jnp.broadcast_to(flags, (8, 128))

    def move(t, carry):
        base = pl.multiple_of(t * 16, 16)
        far = [vrecv[pl.ds(base, 8), :], vrecv[pl.ds(base + 8, 8), :]]
        first_in = None
        for n, tile in enumerate((t, t + HALF)):
            v_x = speed_x(tile)
            v_y = speed_y(tile)
            right = v_x > 0.0
            s_x = jnp.where(right, 1.0, -1.0)
            s_y = jnp.where(v_y > 0.0, 1.0, -1.0)
            a_x = jnp.abs(v_x)
            a_y = jnp.abs(v_y)
            inward = v_y * toward > 0.0
            if n == 0:
                first_in = inward
                halo = far
            else:
                halo = [jnp.where(first_in, f, mirror(f, low_pair)) for f in far]
            cw, gxw, gyw = (comp(tile, k, wall) for k in range(3))
            ci, gxi, gyi = (comp(tile, k, inner) for k in range(3))
            fw = cw + s_y * gyw
            fi = ci + s_y * gyi
            u_w = (
                jnp.where(inward, flag * mirror(fw, low_pair), fi),
                jnp.where(inward, flag * mirror(gxw, low_pair), gxi),
            )
            u_i = (jnp.where(inward, fw, halo[0]), jnp.where(inward, gxw, halo[1]))
            outermost = lane == jnp.where(right, 0, 127)
            for y, c, g_x, g_y, f_y, (uy0, uy1) in (
                (wall, cw, gxw, gyw, fw, u_w),
                (inner, ci, gxi, gyi, fi, u_i),
            ):
                f_x = c + s_x * g_x
                at = pl.multiple_of((tile * 4 + y * 2) * 8, 8)
                e0 = edges[pl.ds(at, 8), :]
                e1 = edges[pl.ds(at + 8, 8), :]
                ux0 = jnp.where(right, pltpu.roll(f_x, 1, 1), pltpu.roll(f_x, 127, 1))
                ux2 = jnp.where(right, pltpu.roll(g_y, 1, 1), pltpu.roll(g_y, 127, 1))
                ux0 = jnp.where(outermost, e0, ux0)
                ux2 = jnp.where(outermost, e1, ux2)
                c2 = c + c
                mean = a_x * (f_x - ux0) + a_y * (f_y - uy0) + c2
                rx = 3.0 * v_x * (f_x + ux0 - c2) + a_y * (g_x - uy1) + 2.0 * g_x
                ry = a_x * (g_y - ux2) + 3.0 * v_y * (f_y + uy0 - c2) + 2.0 * g_y
                for k, value in enumerate((mean, rx, ry)):
                    at = pl.multiple_of((tile * 6 + k * 2 + y) * 8, 8)
                    tb[pl.ds(at, 8), :] = value
        return carry

    lax.fori_loop(0, HALF, move, 0, unroll=2)

    for copy in second:
        copy.wait_recv()
    upper = sub >= 4
    q_of = lax.rem(sub, 4)
    xi = jnp.where(q_of >= 2, GAUSS, -GAUSS)
    eta = jnp.where(lax.rem(q_of, 2) == 1, GAUSS, -GAUSS)

    def moment(k):
        s, n = divmod(k, 10)
        coefs = []
        for j in range(6):
            c = s * 6 + j
            at = c * 8 + n if n < 8 else (12 + c // 4) * 8 + (c % 4) * 2 + n - 8
            coefs.append(jnp.broadcast_to(tot[pl.ds(at, 1), :], (8, 128)))
        a, b, c = (jnp.where(upper, coefs[2 * m + 1], coefs[2 * m]) for m in range(3))
        return a + xi * b + eta * c

    expo, fact = gauss_coefs([moment(k) for k in range(20)])
    for half, coefs in enumerate((expo, fact)):
        for k, x in enumerate(coefs):
            for n, piece in enumerate(split3(x)):
                for r in (k,) if k < 4 else (k, k + 6):
                    cs[pl.ds(half * 384 + n * 16 + r, 8, stride=48), :] = piece
    for i in range(8):
        csb[i, 0:48, 0:128] = cs[i * 48 : i * 48 + 48, :].astype(BF16)
        csb[i, 0:48, 128:256] = cs[384 + i * 48 : 384 + i * 48 + 48, :].astype(BF16)
    for copy in first + second + [send_y, send_e, send_w]:
        copy.wait_send()


def collide(tb, mg, csb, out_hbm, eq, ob, osem):
    for i in range(8):
        eq[i] = jnp.dot(mg[...], csb[i], preferred_element_type=F32)

    stores = []
    quarter = TILES // 4
    for part_no in range(4):
        def finish(t, carry):
            rows8 = pl.ds(pl.multiple_of(t * 8, 8), 8)
            for y in range(2):
                g = [jnp.exp2(eq[y * 4 + q, rows8, 0:128]) * eq[y * 4 + q, rows8, 128:256] for q in range(4)]
                low = g[0] + g[1]
                high = g[2] + g[3]
                vals = (
                    low + high,
                    (3.0 * GAUSS) * (high - low),
                    (3.0 * GAUSS) * ((g[1] - g[0]) + (g[3] - g[2])),
                )
                for k in range(3):
                    at = pl.multiple_of((t * 6 + k * 2 + y) * 8, 8)
                    ob[pl.ds(t * 48 + k * 2 + y, 8, stride=6), :] = tb[pl.ds(at, 8), :] + vals[k]
            return carry

        lax.fori_loop(part_no * quarter, (part_no + 1) * quarter, finish, 0, unroll=4)
        begin = part_no * quarter * 48
        size = min(quarter * 48, ROWS - begin)
        store = pltpu.make_async_copy(ob.at[pl.ds(begin, size)], out_hbm.at[pl.ds(begin, size)], osem.at[part_no])
        store.start()
        stores.append(store)
    for store in stores:
        store.wait()


def shards(state, tangent, orient, walls):
    hbm = pl.BlockSpec(memory_space=pltpu.HBM)
    vmem = pl.BlockSpec(memory_space=pltpu.VMEM)
    tb, mg, csb = pl.pallas_call(
        gather,
        out_shape=(
            pltpu.VMEM((PAD_ROWS, 128), F32),
            pltpu.VMEM((PAD, 128), BF16),
            pltpu.VMEM((8, 128, 256), BF16),
        ),
        in_specs=[hbm] * 4,
        out_specs=[vmem] * 3,
        scratch_shapes=[
            pltpu.VMEM((PAD_ROWS, 128), F32),
            pltpu.VMEM((PAD_ROWS, 128), F32),
            pltpu.VMEM((2, SLOTS), jnp.int32),
            pltpu.VMEM((2, PAD), F32),
            pltpu.VMEM((2, 128), jnp.int32),
            pltpu.VMEM((32, PAD), BF16),
            pltpu.VMEM((PAD, 256), F32),
            pltpu.VMEM((6, 3, PAD, 256), BF16),
            pltpu.VMEM((128, 128), F32),
            pltpu.VMEM((120, 128), F32),
            pltpu.VMEM((8, 128), F32),
            pltpu.VMEM((128, 128), F32),
            pltpu.VMEM((HALF * 16, 128), F32),
            pltpu.VMEM((HALF * 16, 128), F32),
            pltpu.VMEM((16, 128), F32),
            pltpu.VMEM((16, 128), F32),
            pltpu.VMEM((16, 128), F32),
            pltpu.VMEM((TILES * 32, 128), F32),
            pltpu.VMEM((16 * 48, 128), F32),
            pltpu.SemaphoreType.DMA((4,)),
            pltpu.SemaphoreType.DMA((15,)),
            pltpu.SemaphoreType.DMA((15,)),
            pltpu.SemaphoreType.DMA((15,)),
            pltpu.SemaphoreType.DMA((15,)),
            pltpu.SemaphoreType.DMA((2,)),
            pltpu.SemaphoreType.DMA((2,)),
            pltpu.SemaphoreType.DMA((2,)),
        ],
        compiler_params=pltpu.CompilerParams(
            collective_id=0, has_side_effects=True, vmem_limit_bytes=58 * 1024 * 1024
        ),
    )(
        state.reshape(ROWS, 128),
        tangent.reshape(ROWS, 128),
        orient.T,
        walls,
    )
    out = pl.pallas_call(
        collide,
        out_shape=jax.ShapeDtypeStruct((ROWS, 128), F32),
        in_specs=[vmem] * 3,
        out_specs=hbm,
        scratch_shapes=[
            pltpu.VMEM((8, PAD, 256), F32),
            pltpu.VMEM((PAD_ROWS, 128), F32),
            pltpu.SemaphoreType.DMA((4,)),
        ],
        compiler_params=pltpu.CompilerParams(vmem_limit_bytes=16 * 1024 * 1024),
    )(tb, mg, csb)
    return out.reshape(SLOTS, 3, 2, 128)


def solution(mesh):
    placed = (
        P("vert", None, "gy", "gx"),
        P("vert", None, "gy", "gx"),
        P("vert", None),
        P(None, "gx"),
    )
    return jax.shard_map(
        shards, mesh=mesh, in_specs=placed, out_specs=P("vert", None, "gy", "gx"), check_vma=False
    )
```

```python
import functools
import math

import jax
import jax.numpy as jnp
from jax import lax
from jax.experimental import pallas as pl
from jax.experimental.pallas import tpu as pltpu
from jax.sharding import PartitionSpec as P

MESH = pl.DeviceIdType.MESH
F32 = jnp.float32
BF16 = jnp.bfloat16

SLOTS = 500
PAD = 512
TILES = PAD // 8
HALF = TILES // 2
ROWS = SLOTS * 6
PAD_ROWS = PAD * 6
GAUSS = 0.5773502691896258
LOG_TWO_PI = math.log(2.0 * math.pi)
LOG2E = math.log2(math.e)
DUOS = ((0, 0), (1, 1), (2, 2), (0, 1), (0, 2), (1, 2))
PEERS = 16
PARTS = 4
ORDER = (8, 7, 9, 6, 10, 5, 11, 4, 12, 3, 13, 2, 14, 1, 15)


def full(entries):
    rows = [[None] * 3 for _ in range(3)]
    for n, (a, b) in enumerate(DUOS):
        rows[a][b] = entries[n]
        rows[b][a] = entries[n]
    return rows


def gauss_coefs(mom):
    rho = mom[0]
    inv_rho = 1.0 / rho
    u = [mom[1 + a] * inv_rho for a in range(3)]
    sec = mom[4:10]
    theta = [sec[n] * inv_rho - u[a] * u[b] for n, (a, b) in enumerate(DUOS)]
    temp = (theta[0] + theta[1] + theta[2]) * (1.0 / 3.0)
    tn = [(1.5 * temp if a == b else 0.0) - 0.5 * theta[n] for n, (a, b) in enumerate(DUOS)]
    t = full(tn)
    cof = [
        t[1][1] * t[2][2] - t[1][2] * t[1][2],
        t[0][0] * t[2][2] - t[0][2] * t[0][2],
        t[0][0] * t[1][1] - t[0][1] * t[0][1],
        t[0][2] * t[1][2] - t[0][1] * t[2][2],
        t[0][1] * t[1][2] - t[0][2] * t[1][1],
        t[0][1] * t[0][2] - t[0][0] * t[1][2],
    ]
    det = t[0][0] * cof[0] + t[0][1] * cof[3] + t[0][2] * cof[4]
    inv_det = 1.0 / det
    inv = [c * inv_det for c in cof]
    log_pre = jnp.log(rho) - 1.5 * LOG_TWO_PI - 0.5 * jnp.log(det)
    drho = mom[10]
    du = [(mom[11 + a] - u[a] * drho) * inv_rho for a in range(3)]
    dlog = drho * inv_rho
    dtheta = [
        (mom[14 + n] - sec[n] * dlog) * inv_rho - (du[a] * u[b] + u[a] * du[b])
        for n, (a, b) in enumerate(DUOS)
    ]
    dtemp = (dtheta[0] + dtheta[1] + dtheta[2]) * (1.0 / 3.0)
    dtn = [(1.5 * dtemp if a == b else 0.0) - 0.5 * dtheta[n] for n, (a, b) in enumerate(DUOS)]
    A = full(inv)
    D = full(dtn)
    trace = sum(A[a][b] * D[b][a] for a in range(3) for b in range(3))
    shift = dlog - 0.5 * trace
    w = [A[a][0] * du[0] + A[a][1] * du[1] + A[a][2] * du[2] for a in range(3)]
    AD = [[A[a][0] * D[0][c] + A[a][1] * D[1][c] + A[a][2] * D[2][c] for c in range(3)] for a in range(3)]
    curve = [AD[a][0] * A[0][b] + AD[a][1] * A[1][b] + AD[a][2] * A[2][b] for a, b in DUOS]
    B = full(curve)
    au = [A[a][0] * u[0] + A[a][1] * u[1] + A[a][2] * u[2] for a in range(3)]
    bu = [B[a][0] * u[0] + B[a][1] * u[1] + B[a][2] * u[2] for a in range(3)]
    e0 = log_pre - 0.5 * (u[0] * au[0] + u[1] * au[1] + u[2] * au[2])
    expo = [e0] + au + [-0.5 * inv[n] if n < 3 else -inv[n] for n in range(6)]
    q0 = shift - (u[0] * w[0] + u[1] * w[1] + u[2] * w[2]) + 0.5 * (u[0] * bu[0] + u[1] * bu[1] + u[2] * bu[2])
    fact = [q0] + [w[a] - bu[a] for a in range(3)] + [0.5 * curve[n] if n < 3 else curve[n] for n in range(6)]
    return [x * LOG2E for x in expo], [x * -0.5 for x in fact]


def split3(x):
    hi = x.astype(BF16).astype(F32)
    r = x - hi
    mid = r.astype(BF16).astype(F32)
    return hi, mid, r - mid


def mirror(x, low_pair):
    return jnp.where(low_pair, pltpu.roll(x, 6, 0), pltpu.roll(x, 2, 0))


def gather(
    state_hbm, tan_hbm, orient_hbm, walls_hbm, tb, mg, csb,
    xs, xt, orient_v, bits, walls_v, ml, vxy, xsp, part, rx1, sumt, tot,
    vsend, relay, vrecv, xsend, xleft, xright, edges, cs,
    lsem, s1, r1, s2, r2, ysem, xsem_s, xsem_r,
):
    me = lax.axis_index("vert")
    gx = lax.axis_index("gx")
    gy = lax.axis_index("gy")
    wall = gy
    inner = 1 - gy
    load_t = pltpu.make_async_copy(tan_hbm, xt.at[pl.ds(0, ROWS)], lsem.at[0])
    load_s = pltpu.make_async_copy(state_hbm, xs.at[pl.ds(0, ROWS)], lsem.at[1])
    load_o = pltpu.make_async_copy(orient_hbm, orient_v, lsem.at[2])
    load_w = pltpu.make_async_copy(walls_hbm, walls_v, lsem.at[3])
    load_o.start()
    load_t.start()
    load_s.start()
    load_w.start()

    barrier = pltpu.get_barrier_semaphore()
    for d in ORDER:
        pl.semaphore_signal(barrier, inc=1, device_id={"vert": lax.rem(me + d, PEERS)}, device_id_type=MESH)
    odd = lax.rem(gx, 2)
    side = gx + 1 - 2 * odd
    plus = {"gx": side, "gy": lax.rem(gy + odd, 2)}
    minus = {"gx": side, "gy": lax.rem(gy + odd + 1, 2)}
    pl.semaphore_signal(barrier, inc=1, device_id={"gx": side, "gy": inner}, device_id_type=MESH)
    east = lax.rem(gx + 1, 8)
    west = lax.rem(gx + 7, 8)
    pl.semaphore_signal(barrier, inc=1, device_id={"gx": east}, device_id_type=MESH)
    pl.semaphore_signal(barrier, inc=1, device_id={"gx": west}, device_id_type=MESH)

    zeros_tail = jnp.zeros((PAD_ROWS - ROWS, 128), F32)
    xs[pl.ds(ROWS, PAD_ROWS - ROWS), :] = zeros_tail
    xt[pl.ds(ROWS, PAD_ROWS - ROWS), :] = zeros_tail
    bits[...] = jnp.zeros((2, PAD), F32)
    load_o.wait()
    bits[:, 0:SLOTS] = orient_v[...].astype(F32)
    row = lax.broadcasted_iota(jnp.int32, (8, PAD), 0)
    slot = (lax.broadcasted_iota(jnp.int32, (8, PAD), 1) + me * SLOTS).astype(F32) + 0.5
    by40 = jnp.floor(slot * (1.0 / 40.0))
    by400 = jnp.floor(slot * (1.0 / 400.0))
    by4 = jnp.floor(slot * 0.25)
    sx = jnp.broadcast_to(bits[0:1, :], (8, PAD)) * 2.0 - 1.0
    sy = jnp.broadcast_to(bits[1:2, :], (8, PAD)) * 2.0 - 1.0
    vx = sx * (by40 - 10.0 * by400 + 0.5) * 0.5
    vy = sy * (by4 - 10.0 * by40 + 0.5) * 0.5
    vz = (by400 - 9.5) * 0.5
    quad = [vx * vx, vy * vy, vz * vz, vx * vy, vx * vz, vy * vz]
    qhi = [q.astype(BF16).astype(F32) for q in quad]
    qlo = [q - h for q, h in zip(quad, qhi)]
    lin = [jnp.ones((8, PAD), F32), vx, vy, vz]
    zero = jnp.zeros((8, PAD), F32)

    def pick(values):
        out = values[0]
        for k in range(1, 8):
            out = jnp.where(row == k, values[k], out)
        return out

    head = pick(lin + qhi[:4])
    tail = pick(qhi[4:] + qlo)
    lows = pick([zero] * 4 + qlo[:4])
    even = lax.rem(row, 2) == 0
    pair_hi = jnp.where(even, qhi[4], qhi[5])
    pair_lo = jnp.where(even, qlo[4], qlo[5])
    ml[...] = (jnp.concatenate([head, lows, pair_hi, pair_lo], axis=0) * 0.125).astype(BF16)
    table = jnp.concatenate([head, tail] * 3 + [zero] * 10, axis=0)
    mg[...] = jnp.transpose(table).astype(BF16)
    krow = lax.broadcasted_iota(jnp.int32, (128, 256), 0)
    kcol = lax.broadcasted_iota(jnp.int32, (128, 256), 1)
    choose = jnp.where(krow == 1 + (kcol >> 7), 1.0, 0.0).astype(BF16)
    vxy[...] = jnp.dot(mg[...], choose, preferred_element_type=F32)
    csb[...] = jnp.zeros(csb.shape, BF16)

    sub = lax.broadcasted_iota(jnp.int32, (8, 128), 0)
    lane = lax.broadcasted_iota(jnp.int32, (8, 128), 1)
    low_pair = lax.rem(sub, 4) < 2
    toward = (1 - 2 * gy).astype(F32)

    def comp(tile, coef, y):
        return xt[pl.ds(tile * 48 + coef * 2 + y, 8, stride=6), :]

    def speed_x(tile):
        return vxy[pl.ds(pl.multiple_of(tile * 8, 8), 8), 0:128]

    def speed_y(tile):
        return vxy[pl.ds(pl.multiple_of(tile * 8, 8), 8), 128:256]

    load_t.wait()

    def pack_rows(t, carry):
        traces = []
        for tile in (t, t + HALF):
            v = speed_y(tile)
            sgn = jnp.where(v > 0.0, 1.0, -1.0)
            value = comp(tile, 0, inner) + sgn * comp(tile, 2, inner)
            traces.append((v * toward > 0.0, value, comp(tile, 1, inner)))
        (in0, val0, slo0), (in1, val1, slo1) = traces
        base = pl.multiple_of(t * 16, 16)
        vsend[pl.ds(base, 8), :] = jnp.where(in0, val0, jnp.where(in1, val1, mirror(val1, low_pair)))
        vsend[pl.ds(base + 8, 8), :] = jnp.where(in0, slo0, jnp.where(in1, slo1, mirror(slo1, low_pair)))
        return carry

    lax.fori_loop(0, HALF, pack_rows, 0, unroll=4)

    def spread(ref, first):
        def body(t, carry):
            for j in range(6):
                hi, mid, lo = split3(ref[pl.ds(t * 96 + j, 16, stride=6), :])
                rows16 = pl.ds(pl.multiple_of(t * 16, 16), 16)
                cols = pl.ds((j % 2) * 128, 128)
                xsp[first + j // 2, 0, rows16, cols] = hi.astype(BF16)
                xsp[first + j // 2, 1, rows16, cols] = mid.astype(BF16)
                xsp[first + j // 2, 2, rows16, cols] = lo.astype(BF16)
            return carry

        lax.fori_loop(0, PAD // 16, body, 0)

    spread(xt, 3)
    pl.semaphore_wait(barrier, PEERS + 2)
    halves = (pl.ds(0, HALF * 8), pl.ds(HALF * 8, HALF * 8))
    hop1 = [
        pltpu.make_async_remote_copy(
            src_ref=vsend.at[halves[n]], dst_ref=relay.at[halves[n]], send_sem=ysem.at[0, n], recv_sem=ysem.at[1, n],
            device_id=to, device_id_type=MESH,
        )
        for n, to in enumerate((plus, minus))
    ]
    hop2 = [
        pltpu.make_async_remote_copy(
            src_ref=relay.at[halves[n]], dst_ref=vrecv.at[halves[n]], send_sem=ysem.at[2, n], recv_sem=ysem.at[3, n],
            device_id=to, device_id_type=MESH,
        )
        for n, to in enumerate((plus, minus))
    ]
    for copy in hop1:
        copy.start()
    load_s.wait()
    spread(xs, 0)
    group = sub // 2
    packed = [None] * 3
    for p in range(6):
        acc = jnp.dot(ml[...], xsp[p, 0], preferred_element_type=F32)
        acc += jnp.dot(ml[...], xsp[p, 1], preferred_element_type=F32)
        acc += jnp.dot(ml[...], xsp[p, 2], preferred_element_type=F32)
        for h in range(2):
            c = 2 * p + h
            cols = slice(h * 128, h * 128 + 128)
            part[pl.ds(c * 8, 8), :] = acc[0:8, cols] + acc[8:16, cols]
            extra = acc[16:24, cols] + acc[24:32, cols]
            old = packed[c // 4]
            packed[c // 4] = extra if old is None else jnp.where(group == c % 4, extra, old)
    for i in range(3):
        part[pl.ds((12 + i) * 8, 8), :] = packed[i]
    part[pl.ds(120, 8), :] = jnp.zeros((8, 128), F32)

    first = []
    for d in ORDER:
        peer = lax.rem(me + d, PEERS)
        copy = pltpu.make_async_remote_copy(
            src_ref=part.at[pl.ds(pl.multiple_of(peer * 8, 8), 8)],
            dst_ref=rx1.at[pl.ds((15 - d) * 8, 8)],
            send_sem=s1.at[d - 1], recv_sem=r1.at[d - 1],
            device_id={"vert": peer}, device_id_type=MESH,
        )
        copy.start()
        first.append(copy)

    def pack_cols(v, carry):
        acc = jnp.zeros((8, 128), F32)
        for n in range(HALF):
            tile = v * HALF + n
            right = speed_x(tile) > 0.0
            sgn = jnp.where(right, 1.0, -1.0)
            for y in range(2):
                value = comp(tile, 0, y) + sgn * comp(tile, 1, y)
                for k, x in enumerate((value, comp(tile, 2, y))):
                    at = n * 4 + y * 2 + k
                    moved = jnp.where(right, pltpu.roll(x, (at + 1) % 128, 1), pltpu.roll(x, at, 1) if at else x)
                    acc = jnp.where(lane == at, moved, acc)
        xsend[pl.ds(pl.multiple_of(v * 8, 8), 8), :] = acc
        return carry

    lax.fori_loop(0, 2, pack_cols, 0)
    send_e = pltpu.make_async_remote_copy(
        src_ref=xsend, dst_ref=xleft, send_sem=xsem_s.at[0], recv_sem=xsem_r.at[0],
        device_id={"gx": east}, device_id_type=MESH,
    )
    send_w = pltpu.make_async_remote_copy(
        src_ref=xsend, dst_ref=xright, send_sem=xsem_s.at[1], recv_sem=xsem_r.at[1],
        device_id={"gx": west}, device_id_type=MESH,
    )
    send_e.start()
    send_w.start()

    for came, goes in zip(hop1, hop2):
        came.wait_recv()
        goes.start()

    for copy in first:
        copy.wait_recv()
    mine = pl.ds(pl.multiple_of(me * 8, 8), 8)
    total = part[mine, :]
    for k in range(15):
        total = total + rx1[pl.ds(k * 8, 8), :]
    sumt[...] = total
    tot[mine, :] = total
    second = []
    for d in ORDER:
        copy = pltpu.make_async_remote_copy(
            src_ref=sumt, dst_ref=tot.at[mine],
            send_sem=s2.at[d - 1], recv_sem=r2.at[d - 1],
            device_id={"vert": lax.rem(me + d, PEERS)}, device_id_type=MESH,
        )
        copy.start()
        second.append(copy)

    send_e.wait_recv()
    send_w.wait_recv()

    def unpack_cols(v, carry):
        rows8 = pl.ds(pl.multiple_of(v * 8, 8), 8)
        west_in = xleft[rows8, :]
        east_in = xright[rows8, :]
        for n in range(HALF):
            tile = v * HALF + n
            right = speed_x(tile) > 0.0
            for k in range(4):
                at = slice(n * 4 + k, n * 4 + k + 1)
                value = jnp.where(right, jnp.broadcast_to(west_in[:, at], (8, 128)), jnp.broadcast_to(east_in[:, at], (8, 128)))
                edges[pl.ds(pl.multiple_of((tile * 4 + k) * 8, 8), 8), :] = value
        return carry

    lax.fori_loop(0, 2, unpack_cols, 0)
    load_w.wait()
    flags = walls_v[pl.ds(wall, 1), :].astype(F32)
    flag = jnp.broadcast_to(flags, (8, 128))

    def move(t, carry):
        for tile in (t, t + HALF):
            v_x = speed_x(tile)
            v_y = speed_y(tile)
            right = v_x > 0.0
            s_x = jnp.where(right, 1.0, -1.0)
            s_y = jnp.where(v_y > 0.0, 1.0, -1.0)
            a_x = jnp.abs(v_x)
            a_y = jnp.abs(v_y)
            inward = v_y * toward > 0.0
            cw, gxw, gyw = (comp(tile, k, wall) for k in range(3))
            ci, gxi, gyi = (comp(tile, k, inner) for k in range(3))
            fw = cw + s_y * gyw
            fi = ci + s_y * gyi
            u_w = (
                jnp.where(inward, flag * mirror(fw, low_pair), fi),
                jnp.where(inward, flag * mirror(gxw, low_pair), gxi),
            )
            u_i = (jnp.where(inward, fw, 0.0), jnp.where(inward, gxw, 0.0))
            outermost = lane == jnp.where(right, 0, 127)
            for y, c, g_x, g_y, f_y, (uy0, uy1) in (
                (wall, cw, gxw, gyw, fw, u_w),
                (inner, ci, gxi, gyi, fi, u_i),
            ):
                f_x = c + s_x * g_x
                at = pl.multiple_of((tile * 4 + y * 2) * 8, 8)
                e0 = edges[pl.ds(at, 8), :]
                e1 = edges[pl.ds(at + 8, 8), :]
                ux0 = jnp.where(right, pltpu.roll(f_x, 1, 1), pltpu.roll(f_x, 127, 1))
                ux2 = jnp.where(right, pltpu.roll(g_y, 1, 1), pltpu.roll(g_y, 127, 1))
                ux0 = jnp.where(outermost, e0, ux0)
                ux2 = jnp.where(outermost, e1, ux2)
                c2 = c + c
                mean = a_x * (f_x - ux0) + a_y * (f_y - uy0) + c2
                rx = 3.0 * v_x * (f_x + ux0 - c2) + a_y * (g_x - uy1) + 2.0 * g_x
                ry = a_x * (g_y - ux2) + 3.0 * v_y * (f_y + uy0 - c2) + 2.0 * g_y
                for k, value in enumerate((mean, rx, ry)):
                    at = pl.multiple_of((tile * 6 + k * 2 + y) * 8, 8)
                    tb[pl.ds(at, 8), :] = value
        return carry

    lax.fori_loop(0, HALF, move, 0, unroll=2)

    for copy in hop2:
        copy.wait_recv()

    def add_halo(t, carry):
        base = pl.multiple_of(t * 16, 16)
        near = [vrecv[pl.ds(base, 8), :], vrecv[pl.ds(base + 8, 8), :]]
        first_in = speed_y(t) * toward > 0.0
        for tile in (t, t + HALF):
            v_y = speed_y(tile)
            speed = jnp.where(v_y * toward > 0.0, 0.0, v_y)
            value, slope = near if tile is t else [jnp.where(first_in, f, mirror(f, low_pair)) for f in near]
            a_y = jnp.abs(speed)
            for k, term in enumerate((-a_y * value, -a_y * slope, 3.0 * speed * value)):
                at = pl.ds(pl.multiple_of((tile * 6 + k * 2 + inner) * 8, 8), 8)
                tb[at, :] = tb[at, :] + term
        return carry

    lax.fori_loop(0, HALF, add_halo, 0, unroll=4)

    for copy in second:
        copy.wait_recv()
    upper = sub >= 4
    q_of = lax.rem(sub, 4)
    xi = jnp.where(q_of >= 2, GAUSS, -GAUSS)
    eta = jnp.where(lax.rem(q_of, 2) == 1, GAUSS, -GAUSS)

    def moment(k):
        s, n = divmod(k, 10)
        coefs = []
        for j in range(6):
            c = s * 6 + j
            at = c * 8 + n if n < 8 else (12 + c // 4) * 8 + (c % 4) * 2 + n - 8
            coefs.append(jnp.broadcast_to(tot[pl.ds(at, 1), :], (8, 128)))
        a, b, c = (jnp.where(upper, coefs[2 * m + 1], coefs[2 * m]) for m in range(3))
        return a + xi * b + eta * c

    expo, fact = gauss_coefs([moment(k) for k in range(20)])
    for half, coefs in enumerate((expo, fact)):
        for k, x in enumerate(coefs):
            for n, piece in enumerate(split3(x)):
                for r in (k,) if k < 4 else (k, k + 6):
                    cs[pl.ds(half * 384 + n * 16 + r, 8, stride=48), :] = piece
    for i in range(8):
        csb[i, 0:48, 0:128] = cs[i * 48 : i * 48 + 48, :].astype(BF16)
        csb[i, 0:48, 128:256] = cs[384 + i * 48 : 384 + i * 48 + 48, :].astype(BF16)
    for copy in first + second + hop1 + hop2 + [send_e, send_w]:
        copy.wait_send()


def collide(tb, mg, csb, out_hbm, eq, ob, osem):
    stores = []
    tiles = TILES // PARTS
    for n in range(PARTS):
        rows = slice(n * tiles * 8, (n + 1) * tiles * 8)
        for i in range(8):
            eq[i, rows, :] = jnp.dot(mg[rows, :], csb[i], preferred_element_type=F32)
        for t in range(n * tiles, (n + 1) * tiles):
            rows8 = slice(t * 8, t * 8 + 8)
            for y in range(2):
                g = [jnp.exp2(eq[y * 4 + q, rows8, 0:128]) * eq[y * 4 + q, rows8, 128:256] for q in range(4)]
                low = g[0] + g[1]
                high = g[2] + g[3]
                vals = (
                    low + high,
                    (3.0 * GAUSS) * (high - low),
                    (3.0 * GAUSS) * ((g[1] - g[0]) + (g[3] - g[2])),
                )
                for k in range(3):
                    at = (t * 6 + k * 2 + y) * 8
                    ob[pl.ds(t * 48 + k * 2 + y, 8, stride=6), :] = tb[at : at + 8, :] + vals[k]
        begin = n * tiles * 48
        size = min(tiles * 48, ROWS - begin)
        store = pltpu.make_async_copy(ob.at[pl.ds(begin, size)], out_hbm.at[pl.ds(begin, size)], osem.at[n])
        store.start()
        stores.append(store)
    for store in stores:
        store.wait()


def shards(state, tangent, orient, walls):
    hbm = pl.BlockSpec(memory_space=pltpu.HBM)
    vmem = pl.BlockSpec(memory_space=pltpu.VMEM)
    tb, mg, csb = pl.pallas_call(
        gather,
        out_shape=(
            pltpu.VMEM((PAD_ROWS, 128), F32),
            pltpu.VMEM((PAD, 128), BF16),
            pltpu.VMEM((8, 128, 256), BF16),
        ),
        in_specs=[hbm] * 4,
        out_specs=[vmem] * 3,
        scratch_shapes=[
            pltpu.VMEM((PAD_ROWS, 128), F32),
            pltpu.VMEM((PAD_ROWS, 128), F32),
            pltpu.VMEM((2, SLOTS), jnp.int32),
            pltpu.VMEM((2, PAD), F32),
            pltpu.VMEM((2, 128), jnp.int32),
            pltpu.VMEM((32, PAD), BF16),
            pltpu.VMEM((PAD, 256), F32),
            pltpu.VMEM((6, 3, PAD, 256), BF16),
            pltpu.VMEM((128, 128), F32),
            pltpu.VMEM((120, 128), F32),
            pltpu.VMEM((8, 128), F32),
            pltpu.VMEM((128, 128), F32),
            pltpu.VMEM((HALF * 16, 128), F32),
            pltpu.VMEM((HALF * 16, 128), F32),
            pltpu.VMEM((HALF * 16, 128), F32),
            pltpu.VMEM((16, 128), F32),
            pltpu.VMEM((16, 128), F32),
            pltpu.VMEM((16, 128), F32),
            pltpu.VMEM((TILES * 32, 128), F32),
            pltpu.VMEM((16 * 48, 128), F32),
            pltpu.SemaphoreType.DMA((4,)),
            pltpu.SemaphoreType.DMA((15,)),
            pltpu.SemaphoreType.DMA((15,)),
            pltpu.SemaphoreType.DMA((15,)),
            pltpu.SemaphoreType.DMA((15,)),
            pltpu.SemaphoreType.DMA((4, 2)),
            pltpu.SemaphoreType.DMA((2,)),
            pltpu.SemaphoreType.DMA((2,)),
        ],
        compiler_params=pltpu.CompilerParams(
            collective_id=0, has_side_effects=True, vmem_limit_bytes=58 * 1024 * 1024
        ),
    )(
        state.reshape(ROWS, 128),
        tangent.reshape(ROWS, 128),
        orient.T,
        walls,
    )
    out = pl.pallas_call(
        collide,
        out_shape=jax.ShapeDtypeStruct((ROWS, 128), F32),
        in_specs=[vmem] * 3,
        out_specs=hbm,
        scratch_shapes=[
            pltpu.VMEM((8, PAD, 256), F32),
            pltpu.VMEM((PAD_ROWS, 128), F32),
            pltpu.SemaphoreType.DMA((PARTS,)),
        ],
        compiler_params=pltpu.CompilerParams(vmem_limit_bytes=16 * 1024 * 1024),
    )(tb, mg, csb)
    return out.reshape(SLOTS, 3, 2, 128)


def solution(mesh):
    placed = (
        P("vert", None, "gy", "gx"),
        P("vert", None, "gy", "gx"),
        P("vert", None),
        P(None, "gx"),
    )
    return jax.shard_map(
        shards, mesh=mesh, in_specs=placed, out_specs=P("vert", None, "gy", "gx"), check_vma=False
    )
```

```python
import functools
import math

import jax
import jax.numpy as jnp
from jax import lax
from jax.experimental import pallas as pl
from jax.experimental.pallas import tpu as pltpu
from jax.sharding import PartitionSpec as P

MESH = pl.DeviceIdType.MESH
F32 = jnp.float32
BF16 = jnp.bfloat16

SLOTS = 500
PAD = 512
TILES = PAD // 8
HALF = TILES // 2
ROWS = SLOTS * 6
PAD_ROWS = PAD * 6
GAUSS = 0.5773502691896258
LOG_TWO_PI = math.log(2.0 * math.pi)
LOG2E = math.log2(math.e)
DUOS = ((0, 0), (1, 1), (2, 2), (0, 1), (0, 2), (1, 2))
PEERS = 16
PARTS = 4
ORDER = (8, 7, 9, 6, 10, 5, 11, 4, 12, 3, 13, 2, 14, 1, 15)


def full(entries):
    rows = [[None] * 3 for _ in range(3)]
    for n, (a, b) in enumerate(DUOS):
        rows[a][b] = entries[n]
        rows[b][a] = entries[n]
    return rows


def gauss_coefs(mom):
    rho = mom[0]
    inv_rho = 1.0 / rho
    u = [mom[1 + a] * inv_rho for a in range(3)]
    sec = mom[4:10]
    theta = [sec[n] * inv_rho - u[a] * u[b] for n, (a, b) in enumerate(DUOS)]
    temp = (theta[0] + theta[1] + theta[2]) * (1.0 / 3.0)
    tn = [(1.5 * temp if a == b else 0.0) - 0.5 * theta[n] for n, (a, b) in enumerate(DUOS)]
    t = full(tn)
    cof = [
        t[1][1] * t[2][2] - t[1][2] * t[1][2],
        t[0][0] * t[2][2] - t[0][2] * t[0][2],
        t[0][0] * t[1][1] - t[0][1] * t[0][1],
        t[0][2] * t[1][2] - t[0][1] * t[2][2],
        t[0][1] * t[1][2] - t[0][2] * t[1][1],
        t[0][1] * t[0][2] - t[0][0] * t[1][2],
    ]
    det = t[0][0] * cof[0] + t[0][1] * cof[3] + t[0][2] * cof[4]
    inv_det = 1.0 / det
    inv = [c * inv_det for c in cof]
    log_pre = jnp.log(rho) - 1.5 * LOG_TWO_PI - 0.5 * jnp.log(det)
    drho = mom[10]
    du = [(mom[11 + a] - u[a] * drho) * inv_rho for a in range(3)]
    dlog = drho * inv_rho
    dtheta = [
        (mom[14 + n] - sec[n] * dlog) * inv_rho - (du[a] * u[b] + u[a] * du[b])
        for n, (a, b) in enumerate(DUOS)
    ]
    dtemp = (dtheta[0] + dtheta[1] + dtheta[2]) * (1.0 / 3.0)
    dtn = [(1.5 * dtemp if a == b else 0.0) - 0.5 * dtheta[n] for n, (a, b) in enumerate(DUOS)]
    A = full(inv)
    D = full(dtn)
    trace = sum(A[a][b] * D[b][a] for a in range(3) for b in range(3))
    shift = dlog - 0.5 * trace
    w = [A[a][0] * du[0] + A[a][1] * du[1] + A[a][2] * du[2] for a in range(3)]
    AD = [[A[a][0] * D[0][c] + A[a][1] * D[1][c] + A[a][2] * D[2][c] for c in range(3)] for a in range(3)]
    curve = [AD[a][0] * A[0][b] + AD[a][1] * A[1][b] + AD[a][2] * A[2][b] for a, b in DUOS]
    B = full(curve)
    au = [A[a][0] * u[0] + A[a][1] * u[1] + A[a][2] * u[2] for a in range(3)]
    bu = [B[a][0] * u[0] + B[a][1] * u[1] + B[a][2] * u[2] for a in range(3)]
    e0 = log_pre - 0.5 * (u[0] * au[0] + u[1] * au[1] + u[2] * au[2])
    expo = [e0] + au + [-0.5 * inv[n] if n < 3 else -inv[n] for n in range(6)]
    q0 = shift - (u[0] * w[0] + u[1] * w[1] + u[2] * w[2]) + 0.5 * (u[0] * bu[0] + u[1] * bu[1] + u[2] * bu[2])
    fact = [q0] + [w[a] - bu[a] for a in range(3)] + [0.5 * curve[n] if n < 3 else curve[n] for n in range(6)]
    return [x * LOG2E for x in expo], [x * -0.5 for x in fact]


def split3(x):
    hi = x.astype(BF16).astype(F32)
    r = x - hi
    mid = r.astype(BF16).astype(F32)
    return hi, mid, r - mid


def mirror(x, low_pair):
    return jnp.where(low_pair, pltpu.roll(x, 6, 0), pltpu.roll(x, 2, 0))


def gather(
    state_hbm, tan_hbm, orient_hbm, walls_hbm, tb, mg, csb,
    xs, xt, orient_v, bits, walls_v, ml, vxy, part, rx1, sumt, tot,
    vsend, relay, vrecv, xsend, xside, xleft, xright, cs,
    lsem, s1, r1, s2, r2, ysem, xsem_s, xsem_r,
):
    me = lax.axis_index("vert")
    gx = lax.axis_index("gx")
    gy = lax.axis_index("gy")
    wall = gy
    inner = 1 - gy
    load_t = pltpu.make_async_copy(tan_hbm, xt.at[pl.ds(0, ROWS)], lsem.at[0])
    load_s = pltpu.make_async_copy(state_hbm, xs.at[pl.ds(0, ROWS)], lsem.at[1])
    load_o = pltpu.make_async_copy(orient_hbm, orient_v, lsem.at[2])
    load_w = pltpu.make_async_copy(walls_hbm, walls_v, lsem.at[3])
    load_o.start()
    load_t.start()
    load_s.start()
    load_w.start()

    barrier = pltpu.get_barrier_semaphore()
    for d in ORDER:
        pl.semaphore_signal(barrier, inc=1, device_id={"vert": lax.rem(me + d, PEERS)}, device_id_type=MESH)
    odd = lax.rem(gx, 2)
    side = gx + 1 - 2 * odd
    plus = {"gx": side, "gy": lax.rem(gy + odd, 2)}
    minus = {"gx": side, "gy": lax.rem(gy + odd + 1, 2)}
    pl.semaphore_signal(barrier, inc=1, device_id={"gx": side, "gy": inner}, device_id_type=MESH)
    east = lax.rem(gx + 1, 8)
    west = lax.rem(gx + 7, 8)
    pl.semaphore_signal(barrier, inc=1, device_id={"gx": east}, device_id_type=MESH)
    pl.semaphore_signal(barrier, inc=1, device_id={"gx": west}, device_id_type=MESH)

    zeros_tail = jnp.zeros((PAD_ROWS - ROWS, 128), F32)
    xs[pl.ds(ROWS, PAD_ROWS - ROWS), :] = zeros_tail
    xt[pl.ds(ROWS, PAD_ROWS - ROWS), :] = zeros_tail
    bits[...] = jnp.zeros((2, PAD), F32)
    load_o.wait()
    bits[:, 0:SLOTS] = orient_v[...].astype(F32)
    row = lax.broadcasted_iota(jnp.int32, (8, PAD), 0)
    slot = (lax.broadcasted_iota(jnp.int32, (8, PAD), 1) + me * SLOTS).astype(F32) + 0.5
    by40 = jnp.floor(slot * (1.0 / 40.0))
    by400 = jnp.floor(slot * (1.0 / 400.0))
    by4 = jnp.floor(slot * 0.25)
    sx = jnp.broadcast_to(bits[0:1, :], (8, PAD)) * 2.0 - 1.0
    sy = jnp.broadcast_to(bits[1:2, :], (8, PAD)) * 2.0 - 1.0
    vx = sx * (by40 - 10.0 * by400 + 0.5) * 0.5
    vy = sy * (by4 - 10.0 * by40 + 0.5) * 0.5
    vz = (by400 - 9.5) * 0.5
    quad = [vx * vx, vy * vy, vz * vz, vx * vy, vx * vz, vy * vz]
    qhi = [q.astype(BF16).astype(F32) for q in quad]
    qlo = [q - h for q, h in zip(quad, qhi)]
    lin = [jnp.ones((8, PAD), F32), vx, vy, vz]
    zero = jnp.zeros((8, PAD), F32)

    def pick(values):
        out = values[0]
        for k in range(1, 8):
            out = jnp.where(row == k, values[k], out)
        return out

    head = pick(lin + qhi[:4])
    tail = pick(qhi[4:] + qlo)
    lows = pick([zero] * 4 + qlo[:4])
    even = lax.rem(row, 2) == 0
    pair_hi = jnp.where(even, qhi[4], qhi[5])
    pair_lo = jnp.where(even, qlo[4], qlo[5])
    ml[...] = (jnp.concatenate([head, lows, pair_hi, pair_lo], axis=0) * 0.125).astype(BF16)
    table = jnp.concatenate([head, tail] * 3 + [zero] * 10, axis=0)
    mg[...] = jnp.transpose(table).astype(BF16)
    krow = lax.broadcasted_iota(jnp.int32, (128, 256), 0)
    kcol = lax.broadcasted_iota(jnp.int32, (128, 256), 1)
    choose = jnp.where(krow == 1 + (kcol >> 7), 1.0, 0.0).astype(BF16)
    vxy[...] = jnp.dot(mg[...], choose, preferred_element_type=F32)
    csb[...] = jnp.zeros(csb.shape, BF16)

    sub = lax.broadcasted_iota(jnp.int32, (8, 128), 0)
    lane = lax.broadcasted_iota(jnp.int32, (8, 128), 1)
    low_pair = lax.rem(sub, 4) < 2
    toward = (1 - 2 * gy).astype(F32)

    def comp(tile, coef, y):
        return xt[pl.ds(tile * 48 + coef * 2 + y, 8, stride=6), :]

    def speed_x(tile):
        return vxy[pl.ds(pl.multiple_of(tile * 8, 8), 8), 0:128]

    def speed_y(tile):
        return vxy[pl.ds(pl.multiple_of(tile * 8, 8), 8), 128:256]

    load_t.wait()

    def pack_rows(t, carry):
        traces = []
        for tile in (t, t + HALF):
            v = speed_y(tile)
            sgn = jnp.where(v > 0.0, 1.0, -1.0)
            value = comp(tile, 0, inner) + sgn * comp(tile, 2, inner)
            traces.append((v * toward > 0.0, value, comp(tile, 1, inner)))
        (in0, val0, slo0), (in1, val1, slo1) = traces
        base = pl.multiple_of(t * 16, 16)
        vsend[pl.ds(base, 8), :] = jnp.where(in0, val0, jnp.where(in1, val1, mirror(val1, low_pair)))
        vsend[pl.ds(base + 8, 8), :] = jnp.where(in0, slo0, jnp.where(in1, slo1, mirror(slo1, low_pair)))
        return carry

    lax.fori_loop(0, HALF, pack_rows, 0, unroll=4)

    group = sub // 2
    packed = [None] * 3

    def sums(ref, first):
        for p in range(3):
            acc = None
            for k in range(2):
                pair = [ref[pl.ds(k * 1536 + 2 * p + h, 256, stride=6), :] for h in range(2)]
                for piece in split3(jnp.concatenate(pair, axis=1)):
                    got = jnp.dot(ml[:, k * 256 : k * 256 + 256], piece.astype(BF16), preferred_element_type=F32)
                    acc = got if acc is None else acc + got
            for h in range(2):
                c = first + 2 * p + h
                cols = slice(h * 128, h * 128 + 128)
                part[pl.ds(c * 8, 8), :] = acc[0:8, cols] + acc[8:16, cols]
                extra = acc[16:24, cols] + acc[24:32, cols]
                old = packed[c // 4]
                packed[c // 4] = extra if old is None else jnp.where(group == c % 4, extra, old)

    sums(xt, 6)
    load_s.wait()
    sums(xs, 0)
    for i in range(3):
        part[pl.ds((12 + i) * 8, 8), :] = packed[i]
    part[pl.ds(120, 8), :] = jnp.zeros((8, 128), F32)

    pl.semaphore_wait(barrier, PEERS + 2)

    first = []
    for d in ORDER:
        peer = lax.rem(me + d, PEERS)
        copy = pltpu.make_async_remote_copy(
            src_ref=part.at[pl.ds(pl.multiple_of(lax.rem(peer, 8) * 16, 16), 16)],
            dst_ref=rx1.at[pl.ds((15 - d) * 16, 16)],
            send_sem=s1.at[d - 1], recv_sem=r1.at[d - 1],
            device_id={"vert": peer}, device_id_type=MESH,
        )
        copy.start()
        first.append(copy)

    halves = (pl.ds(0, HALF * 8), pl.ds(HALF * 8, HALF * 8))
    hop1 = [
        pltpu.make_async_remote_copy(
            src_ref=vsend.at[halves[n]], dst_ref=relay.at[halves[n]], send_sem=ysem.at[0, n], recv_sem=ysem.at[1, n],
            device_id=to, device_id_type=MESH,
        )
        for n, to in enumerate((plus, minus))
    ]
    hop2 = [
        pltpu.make_async_remote_copy(
            src_ref=relay.at[halves[n]], dst_ref=vrecv.at[halves[n]], send_sem=ysem.at[2, n], recv_sem=ysem.at[3, n],
            device_id=to, device_id_type=MESH,
        )
        for n, to in enumerate((plus, minus))
    ]
    for copy in hop1:
        copy.start()

    quad_lane = lane >> 2

    def pack_cols(v, carry):
        acc = jnp.zeros((8, 128), F32)
        sides = acc
        for n in range(HALF):
            tile = v * HALF + n
            speed = speed_x(tile)
            right = speed > 0.0
            sides = jnp.where(quad_lane == n, speed, sides)
            sgn = jnp.where(right, 1.0, -1.0)
            for y in range(2):
                value = comp(tile, 0, y) + sgn * comp(tile, 1, y)
                for k, x in enumerate((value, comp(tile, 2, y))):
                    at = n * 4 + y * 2 + k
                    moved = jnp.where(right, pltpu.roll(x, (at + 1) % 128, 1), pltpu.roll(x, at, 1) if at else x)
                    acc = jnp.where(lane == at, moved, acc)
        xsend[pl.ds(pl.multiple_of(v * 8, 8), 8), :] = acc
        xside[pl.ds(pl.multiple_of(v * 8, 8), 8), :] = sides
        return carry

    lax.fori_loop(0, 2, pack_cols, 0)
    send_e = pltpu.make_async_remote_copy(
        src_ref=xsend, dst_ref=xleft, send_sem=xsem_s.at[0], recv_sem=xsem_r.at[0],
        device_id={"gx": east}, device_id_type=MESH,
    )
    send_w = pltpu.make_async_remote_copy(
        src_ref=xsend, dst_ref=xright, send_sem=xsem_s.at[1], recv_sem=xsem_r.at[1],
        device_id={"gx": west}, device_id_type=MESH,
    )
    send_e.start()
    send_w.start()

    for came, goes in zip(hop1, hop2):
        came.wait_recv()
        goes.start()

    for copy in first:
        copy.wait_recv()
    chunk = pl.ds(pl.multiple_of(lax.rem(me, 8) * 16, 16), 16)
    total = part[chunk, :]
    for k in range(15):
        total = total + rx1[pl.ds(k * 16, 16), :]
    sumt[...] = total
    tot[chunk, :] = total
    core = lax.rem(me, 2)
    flip = 1 - 2 * core
    second = []
    for k, (chips, other) in enumerate(
        ((2 * flip, 0), (2 * flip, 1), (1, 0), (1, 1), (-1, 0), (-1, 1), (0, 1))
    ):
        copy = pltpu.make_async_remote_copy(
            src_ref=sumt, dst_ref=tot.at[chunk],
            send_sem=s2.at[k], recv_sem=r2.at[k],
            device_id={"vert": lax.rem(me + 2 * chips + other * flip + PEERS, PEERS)}, device_id_type=MESH,
        )
        copy.start()
        second.append(copy)

    load_w.wait()
    flags = walls_v[pl.ds(wall, 1), :].astype(F32)
    flag = jnp.broadcast_to(flags, (8, 128))

    def move(t, carry):
        for tile in (t, t + HALF):
            v_x = speed_x(tile)
            v_y = speed_y(tile)
            right = v_x > 0.0
            s_x = jnp.where(right, 1.0, -1.0)
            s_y = jnp.where(v_y > 0.0, 1.0, -1.0)
            a_x = jnp.abs(v_x)
            a_y = jnp.abs(v_y)
            inward = v_y * toward > 0.0
            cw, gxw, gyw = (comp(tile, k, wall) for k in range(3))
            ci, gxi, gyi = (comp(tile, k, inner) for k in range(3))
            fw = cw + s_y * gyw
            fi = ci + s_y * gyi
            u_w = (
                jnp.where(inward, flag * mirror(fw, low_pair), fi),
                jnp.where(inward, flag * mirror(gxw, low_pair), gxi),
            )
            u_i = (jnp.where(inward, fw, 0.0), jnp.where(inward, gxw, 0.0))
            outermost = lane == jnp.where(right, 0, 127)
            for y, c, g_x, g_y, f_y, (uy0, uy1) in (
                (wall, cw, gxw, gyw, fw, u_w),
                (inner, ci, gxi, gyi, fi, u_i),
            ):
                f_x = c + s_x * g_x
                ux0 = jnp.where(right, pltpu.roll(f_x, 1, 1), pltpu.roll(f_x, 127, 1))
                ux2 = jnp.where(right, pltpu.roll(g_y, 1, 1), pltpu.roll(g_y, 127, 1))
                ux0 = jnp.where(outermost, 0.0, ux0)
                ux2 = jnp.where(outermost, 0.0, ux2)
                c2 = c + c
                mean = a_x * (f_x - ux0) + a_y * (f_y - uy0) + c2
                rx = 3.0 * v_x * (f_x + ux0 - c2) + a_y * (g_x - uy1) + 2.0 * g_x
                ry = a_x * (g_y - ux2) + 3.0 * v_y * (f_y + uy0 - c2) + 2.0 * g_y
                for k, value in enumerate((mean, rx, ry)):
                    at = pl.multiple_of((tile * 6 + k * 2 + y) * 8, 8)
                    tb[pl.ds(at, 8), :] = value
        return carry

    lax.fori_loop(0, HALF, move, 0, unroll=2)

    send_e.wait_recv()
    send_w.wait_recv()

    def add_edges(v, carry):
        rows8 = pl.ds(pl.multiple_of(v * 8, 8), 8)
        came = jnp.where(xside[rows8, :] > 0.0, xleft[rows8, :], xright[rows8, :])
        for n in range(HALF):
            tile = v * HALF + n
            speed = speed_x(tile)
            speed = jnp.where(lane == jnp.where(speed > 0.0, 0, 127), speed, 0.0)
            a_x = jnp.abs(speed)
            for y in range(2):
                value, slope = (
                    jnp.broadcast_to(came[:, n * 4 + y * 2 + k : n * 4 + y * 2 + k + 1], (8, 128)) for k in range(2)
                )
                for k, term in enumerate((-a_x * value, 3.0 * speed * value, -a_x * slope)):
                    at = pl.ds(pl.multiple_of((tile * 6 + k * 2 + y) * 8, 8), 8)
                    tb[at, :] = tb[at, :] + term
        return carry

    lax.fori_loop(0, 2, add_edges, 0)

    for copy in hop2:
        copy.wait_recv()

    def add_halo(t, carry):
        base = pl.multiple_of(t * 16, 16)
        near = [vrecv[pl.ds(base, 8), :], vrecv[pl.ds(base + 8, 8), :]]
        first_in = speed_y(t) * toward > 0.0
        for tile in (t, t + HALF):
            v_y = speed_y(tile)
            speed = jnp.where(v_y * toward > 0.0, 0.0, v_y)
            value, slope = near if tile is t else [jnp.where(first_in, f, mirror(f, low_pair)) for f in near]
            a_y = jnp.abs(speed)
            for k, term in enumerate((-a_y * value, -a_y * slope, 3.0 * speed * value)):
                at = pl.ds(pl.multiple_of((tile * 6 + k * 2 + inner) * 8, 8), 8)
                tb[at, :] = tb[at, :] + term
        return carry

    lax.fori_loop(0, HALF, add_halo, 0, unroll=4)

    for copy in second:
        copy.wait_recv()
    upper = sub >= 4
    q_of = lax.rem(sub, 4)
    xi = jnp.where(q_of >= 2, GAUSS, -GAUSS)
    eta = jnp.where(lax.rem(q_of, 2) == 1, GAUSS, -GAUSS)

    def moment(k):
        s, n = divmod(k, 10)
        coefs = []
        for j in range(6):
            c = s * 6 + j
            at = c * 8 + n if n < 8 else (12 + c // 4) * 8 + (c % 4) * 2 + n - 8
            coefs.append(jnp.broadcast_to(tot[pl.ds(at, 1), :], (8, 128)))
        a, b, c = (jnp.where(upper, coefs[2 * m + 1], coefs[2 * m]) for m in range(3))
        return a + xi * b + eta * c

    expo, fact = gauss_coefs([moment(k) for k in range(20)])
    for half, coefs in enumerate((expo, fact)):
        for k, x in enumerate(coefs):
            for n, piece in enumerate(split3(x)):
                for r in (k,) if k < 4 else (k, k + 6):
                    cs[pl.ds(half * 384 + n * 16 + r, 8, stride=48), :] = piece
    for i in range(8):
        csb[i, 0:48, 0:128] = cs[i * 48 : i * 48 + 48, :].astype(BF16)
        csb[i, 0:48, 128:256] = cs[384 + i * 48 : 384 + i * 48 + 48, :].astype(BF16)
    for copy in first + second + hop1 + hop2 + [send_e, send_w]:
        copy.wait_send()


def collide(tb, mg, csb, out_hbm, eq, ob, osem):
    stores = []
    tiles = TILES // PARTS
    for n in range(PARTS):
        rows = slice(n * tiles * 8, (n + 1) * tiles * 8)
        for i in range(8):
            eq[i, rows, :] = jnp.dot(mg[rows, :], csb[i], preferred_element_type=F32)
        for t in range(n * tiles, (n + 1) * tiles):
            rows8 = slice(t * 8, t * 8 + 8)
            for y in range(2):
                g = [jnp.exp2(eq[y * 4 + q, rows8, 0:128]) * eq[y * 4 + q, rows8, 128:256] for q in range(4)]
                low = g[0] + g[1]
                high = g[2] + g[3]
                vals = (
                    low + high,
                    (3.0 * GAUSS) * (high - low),
                    (3.0 * GAUSS) * ((g[1] - g[0]) + (g[3] - g[2])),
                )
                for k in range(3):
                    at = (t * 6 + k * 2 + y) * 8
                    ob[pl.ds(t * 48 + k * 2 + y, 8, stride=6), :] = tb[at : at + 8, :] + vals[k]
        begin = n * tiles * 48
        size = min(tiles * 48, ROWS - begin)
        store = pltpu.make_async_copy(ob.at[pl.ds(begin, size)], out_hbm.at[pl.ds(begin, size)], osem.at[n])
        store.start()
        stores.append(store)
    for store in stores:
        store.wait()


def shards(state, tangent, orient, walls):
    hbm = pl.BlockSpec(memory_space=pltpu.HBM)
    vmem = pl.BlockSpec(memory_space=pltpu.VMEM)
    tb, mg, csb = pl.pallas_call(
        gather,
        out_shape=(
            pltpu.VMEM((PAD_ROWS, 128), F32),
            pltpu.VMEM((PAD, 128), BF16),
            pltpu.VMEM((8, 128, 256), BF16),
        ),
        in_specs=[hbm] * 4,
        out_specs=[vmem] * 3,
        scratch_shapes=[
            pltpu.VMEM((PAD_ROWS, 128), F32),
            pltpu.VMEM((PAD_ROWS, 128), F32),
            pltpu.VMEM((2, SLOTS), jnp.int32),
            pltpu.VMEM((2, PAD), F32),
            pltpu.VMEM((2, 128), jnp.int32),
            pltpu.VMEM((32, PAD), BF16),
            pltpu.VMEM((PAD, 256), F32),
            pltpu.VMEM((128, 128), F32),
            pltpu.VMEM((240, 128), F32),
            pltpu.VMEM((16, 128), F32),
            pltpu.VMEM((128, 128), F32),
            pltpu.VMEM((HALF * 16, 128), F32),
            pltpu.VMEM((HALF * 16, 128), F32),
            pltpu.VMEM((HALF * 16, 128), F32),
            pltpu.VMEM((16, 128), F32),
            pltpu.VMEM((16, 128), F32),
            pltpu.VMEM((16, 128), F32),
            pltpu.VMEM((16, 128), F32),
            pltpu.VMEM((16 * 48, 128), F32),
            pltpu.SemaphoreType.DMA((4,)),
            pltpu.SemaphoreType.DMA((15,)),
            pltpu.SemaphoreType.DMA((15,)),
            pltpu.SemaphoreType.DMA((15,)),
            pltpu.SemaphoreType.DMA((15,)),
            pltpu.SemaphoreType.DMA((4, 2)),
            pltpu.SemaphoreType.DMA((2,)),
            pltpu.SemaphoreType.DMA((2,)),
        ],
        compiler_params=pltpu.CompilerParams(
            collective_id=0, has_side_effects=True, vmem_limit_bytes=58 * 1024 * 1024
        ),
    )(
        state.reshape(ROWS, 128),
        tangent.reshape(ROWS, 128),
        orient.T,
        walls,
    )
    out = pl.pallas_call(
        collide,
        out_shape=jax.ShapeDtypeStruct((ROWS, 128), F32),
        in_specs=[vmem] * 3,
        out_specs=hbm,
        scratch_shapes=[
            pltpu.VMEM((8, PAD, 256), F32),
            pltpu.VMEM((PAD_ROWS, 128), F32),
            pltpu.SemaphoreType.DMA((PARTS,)),
        ],
        compiler_params=pltpu.CompilerParams(vmem_limit_bytes=16 * 1024 * 1024),
    )(tb, mg, csb)
    return out.reshape(SLOTS, 3, 2, 128)


def solution(mesh):
    placed = (
        P("vert", None, "gy", "gx"),
        P("vert", None, "gy", "gx"),
        P("vert", None),
        P(None, "gx"),
    )
    return jax.shard_map(
        shards, mesh=mesh, in_specs=placed, out_specs=P("vert", None, "gy", "gx"), check_vma=False
    )
```

```python
import functools
import math

import jax
import jax.numpy as jnp
from jax import lax
from jax.experimental import pallas as pl
from jax.experimental.pallas import tpu as pltpu
from jax.sharding import PartitionSpec as P

MESH = pl.DeviceIdType.MESH
F32 = jnp.float32
BF16 = jnp.bfloat16

SLOTS = 500
PAD = 512
TILES = PAD // 8
HALF = TILES // 2
ROWS = SLOTS * 6
PAD_ROWS = PAD * 6
GAUSS = 0.5773502691896258
LOG_TWO_PI = math.log(2.0 * math.pi)
LOG2E = math.log2(math.e)
DUOS = ((0, 0), (1, 1), (2, 2), (0, 1), (0, 2), (1, 2))
PEERS = 16
PARTS = 4
ORDER = (8, 7, 9, 6, 10, 5, 11, 4, 12, 3, 13, 2, 14, 1, 15)


def full(entries):
    rows = [[None] * 3 for _ in range(3)]
    for n, (a, b) in enumerate(DUOS):
        rows[a][b] = entries[n]
        rows[b][a] = entries[n]
    return rows


def gauss_coefs(mom):
    rho = mom[0]
    inv_rho = 1.0 / rho
    u = [mom[1 + a] * inv_rho for a in range(3)]
    sec = mom[4:10]
    theta = [sec[n] * inv_rho - u[a] * u[b] for n, (a, b) in enumerate(DUOS)]
    temp = (theta[0] + theta[1] + theta[2]) * (1.0 / 3.0)
    tn = [(1.5 * temp if a == b else 0.0) - 0.5 * theta[n] for n, (a, b) in enumerate(DUOS)]
    t = full(tn)
    cof = [
        t[1][1] * t[2][2] - t[1][2] * t[1][2],
        t[0][0] * t[2][2] - t[0][2] * t[0][2],
        t[0][0] * t[1][1] - t[0][1] * t[0][1],
        t[0][2] * t[1][2] - t[0][1] * t[2][2],
        t[0][1] * t[1][2] - t[0][2] * t[1][1],
        t[0][1] * t[0][2] - t[0][0] * t[1][2],
    ]
    det = t[0][0] * cof[0] + t[0][1] * cof[3] + t[0][2] * cof[4]
    inv_det = 1.0 / det
    inv = [c * inv_det for c in cof]
    log_pre = jnp.log(rho) - 1.5 * LOG_TWO_PI - 0.5 * jnp.log(det)
    drho = mom[10]
    du = [(mom[11 + a] - u[a] * drho) * inv_rho for a in range(3)]
    dlog = drho * inv_rho
    dtheta = [
        (mom[14 + n] - sec[n] * dlog) * inv_rho - (du[a] * u[b] + u[a] * du[b])
        for n, (a, b) in enumerate(DUOS)
    ]
    dtemp = (dtheta[0] + dtheta[1] + dtheta[2]) * (1.0 / 3.0)
    dtn = [(1.5 * dtemp if a == b else 0.0) - 0.5 * dtheta[n] for n, (a, b) in enumerate(DUOS)]
    A = full(inv)
    D = full(dtn)
    trace = sum(A[a][b] * D[b][a] for a in range(3) for b in range(3))
    shift = dlog - 0.5 * trace
    w = [A[a][0] * du[0] + A[a][1] * du[1] + A[a][2] * du[2] for a in range(3)]
    AD = [[A[a][0] * D[0][c] + A[a][1] * D[1][c] + A[a][2] * D[2][c] for c in range(3)] for a in range(3)]
    curve = [AD[a][0] * A[0][b] + AD[a][1] * A[1][b] + AD[a][2] * A[2][b] for a, b in DUOS]
    B = full(curve)
    au = [A[a][0] * u[0] + A[a][1] * u[1] + A[a][2] * u[2] for a in range(3)]
    bu = [B[a][0] * u[0] + B[a][1] * u[1] + B[a][2] * u[2] for a in range(3)]
    e0 = log_pre - 0.5 * (u[0] * au[0] + u[1] * au[1] + u[2] * au[2])
    expo = [e0] + au + [-0.5 * inv[n] if n < 3 else -inv[n] for n in range(6)]
    q0 = shift - (u[0] * w[0] + u[1] * w[1] + u[2] * w[2]) + 0.5 * (u[0] * bu[0] + u[1] * bu[1] + u[2] * bu[2])
    fact = [q0] + [w[a] - bu[a] for a in range(3)] + [0.5 * curve[n] if n < 3 else curve[n] for n in range(6)]
    return [x * LOG2E for x in expo], [x * -0.5 for x in fact]


def split3(x):
    hi = x.astype(BF16).astype(F32)
    r = x - hi
    mid = r.astype(BF16).astype(F32)
    return hi, mid, r - mid


def mirror(x, low_pair):
    return jnp.where(low_pair, pltpu.roll(x, 6, 0), pltpu.roll(x, 2, 0))


def gather(
    state_hbm, tan_hbm, orient_hbm, walls_hbm, tb, mg, csb,
    xs, xt, orient_v, bits, walls_v, ml, vxy, part, rx1, sumt, tot,
    vsend, relay, vrecv, xsend, xside, xleft, xright, cs,
    lsem, s1, r1, s2, r2, ysem, xsem_s, xsem_r,
):
    me = lax.axis_index("vert")
    gx = lax.axis_index("gx")
    gy = lax.axis_index("gy")
    wall = gy
    inner = 1 - gy
    load_t, load_s = (
        [
            pltpu.make_async_copy(
                hbm.at[pl.ds(k * 1536, size)], ref.at[pl.ds(k * 1536, size)], lsem.at[2 * n + k]
            )
            for k, size in enumerate((1536, ROWS - 1536))
        ]
        for n, (hbm, ref) in enumerate(((tan_hbm, xt), (state_hbm, xs)))
    )
    load_o = pltpu.make_async_copy(orient_hbm, orient_v, lsem.at[4])
    load_w = pltpu.make_async_copy(walls_hbm, walls_v, lsem.at[5])
    load_o.start()
    for copy in load_t + load_s:
        copy.start()
    load_w.start()

    barrier = pltpu.get_barrier_semaphore()
    for d in ORDER:
        pl.semaphore_signal(barrier, inc=1, device_id={"vert": lax.rem(me + d, PEERS)}, device_id_type=MESH)
    odd = lax.rem(gx, 2)
    side = gx + 1 - 2 * odd
    plus = {"gx": side, "gy": lax.rem(gy + odd, 2)}
    minus = {"gx": side, "gy": lax.rem(gy + odd + 1, 2)}
    pl.semaphore_signal(barrier, inc=1, device_id={"gx": side, "gy": inner}, device_id_type=MESH)
    east = lax.rem(gx + 1, 8)
    west = lax.rem(gx + 7, 8)
    pl.semaphore_signal(barrier, inc=1, device_id={"gx": east}, device_id_type=MESH)
    pl.semaphore_signal(barrier, inc=1, device_id={"gx": west}, device_id_type=MESH)

    zeros_tail = jnp.zeros((PAD_ROWS - ROWS, 128), F32)
    xs[pl.ds(ROWS, PAD_ROWS - ROWS), :] = zeros_tail
    xt[pl.ds(ROWS, PAD_ROWS - ROWS), :] = zeros_tail
    bits[...] = jnp.zeros((2, PAD), F32)
    load_o.wait()
    bits[:, 0:SLOTS] = orient_v[...].astype(F32)
    row = lax.broadcasted_iota(jnp.int32, (8, PAD), 0)
    slot = (lax.broadcasted_iota(jnp.int32, (8, PAD), 1) + me * SLOTS).astype(F32) + 0.5
    by40 = jnp.floor(slot * (1.0 / 40.0))
    by400 = jnp.floor(slot * (1.0 / 400.0))
    by4 = jnp.floor(slot * 0.25)
    sx = jnp.broadcast_to(bits[0:1, :], (8, PAD)) * 2.0 - 1.0
    sy = jnp.broadcast_to(bits[1:2, :], (8, PAD)) * 2.0 - 1.0
    vx = sx * (by40 - 10.0 * by400 + 0.5) * 0.5
    vy = sy * (by4 - 10.0 * by40 + 0.5) * 0.5
    vz = (by400 - 9.5) * 0.5
    quad = [vx * vx, vy * vy, vz * vz, vx * vy, vx * vz, vy * vz]
    qhi = [q.astype(BF16).astype(F32) for q in quad]
    qlo = [q - h for q, h in zip(quad, qhi)]
    lin = [jnp.ones((8, PAD), F32), vx, vy, vz]
    zero = jnp.zeros((8, PAD), F32)

    def pick(values):
        out = values[0]
        for k in range(1, 8):
            out = jnp.where(row == k, values[k], out)
        return out

    head = pick(lin + qhi[:4])
    tail = pick(qhi[4:] + qlo)
    lows = pick([zero] * 4 + qlo[:4])
    even = lax.rem(row, 2) == 0
    pair_hi = jnp.where(even, qhi[4], qhi[5])
    pair_lo = jnp.where(even, qlo[4], qlo[5])
    ml[...] = (jnp.concatenate([head, lows, pair_hi, pair_lo], axis=0) * 0.125).astype(BF16)
    table = jnp.concatenate([head, tail] * 3 + [zero] * 10, axis=0)
    mg[...] = jnp.transpose(table).astype(BF16)
    krow = lax.broadcasted_iota(jnp.int32, (128, 256), 0)
    kcol = lax.broadcasted_iota(jnp.int32, (128, 256), 1)
    choose = jnp.where(krow == 1 + (kcol >> 7), 1.0, 0.0).astype(BF16)
    vxy[...] = jnp.dot(mg[...], choose, preferred_element_type=F32)
    csb[...] = jnp.zeros(csb.shape, BF16)

    sub = lax.broadcasted_iota(jnp.int32, (8, 128), 0)
    lane = lax.broadcasted_iota(jnp.int32, (8, 128), 1)
    low_pair = lax.rem(sub, 4) < 2
    toward = (1 - 2 * gy).astype(F32)

    def comp(tile, coef, y):
        return xt[pl.ds(tile * 48 + coef * 2 + y, 8, stride=6), :]

    def speed_x(tile):
        return vxy[pl.ds(pl.multiple_of(tile * 8, 8), 8), 0:128]

    def speed_y(tile):
        return vxy[pl.ds(pl.multiple_of(tile * 8, 8), 8), 128:256]


    group = sub // 2
    packed = [None] * 3

    def sums(ref, first, loads):
        accs = [None] * 3
        for k in range(2):
            loads[k].wait()
            for p in range(3):
                pair = [ref[pl.ds(k * 1536 + 2 * p + h, 256, stride=6), :] for h in range(2)]
                for piece in split3(jnp.concatenate(pair, axis=1)):
                    got = jnp.dot(ml[:, k * 256 : k * 256 + 256], piece.astype(BF16), preferred_element_type=F32)
                    accs[p] = got if accs[p] is None else accs[p] + got
        for p, acc in enumerate(accs):
            for h in range(2):
                c = first + 2 * p + h
                cols = slice(h * 128, h * 128 + 128)
                part[pl.ds(c * 8, 8), :] = acc[0:8, cols] + acc[8:16, cols]
                extra = acc[16:24, cols] + acc[24:32, cols]
                old = packed[c // 4]
                packed[c // 4] = extra if old is None else jnp.where(group == c % 4, extra, old)

    sums(xt, 6, load_t)

    def pack_rows(t, carry):
        traces = []
        for tile in (t, t + HALF):
            v = speed_y(tile)
            sgn = jnp.where(v > 0.0, 1.0, -1.0)
            value = comp(tile, 0, inner) + sgn * comp(tile, 2, inner)
            traces.append((v * toward > 0.0, value, comp(tile, 1, inner)))
        (in0, val0, slo0), (in1, val1, slo1) = traces
        base = pl.multiple_of(t * 16, 16)
        vsend[pl.ds(base, 8), :] = jnp.where(in0, val0, jnp.where(in1, val1, mirror(val1, low_pair)))
        vsend[pl.ds(base + 8, 8), :] = jnp.where(in0, slo0, jnp.where(in1, slo1, mirror(slo1, low_pair)))
        return carry

    lax.fori_loop(0, HALF, pack_rows, 0, unroll=4)

    sums(xs, 0, load_s)
    for i in range(3):
        part[pl.ds((12 + i) * 8, 8), :] = packed[i]
    part[pl.ds(120, 8), :] = jnp.zeros((8, 128), F32)

    pl.semaphore_wait(barrier, PEERS + 2)

    hop1 = []
    hop2 = []
    for n, to in enumerate((plus, minus, plus, minus)):
        piece = pl.ds(n * HALF * 4, HALF * 4)
        hop1.append(pltpu.make_async_remote_copy(
            src_ref=vsend.at[piece], dst_ref=relay.at[piece], send_sem=ysem.at[0, n], recv_sem=ysem.at[1, n],
            device_id=to, device_id_type=MESH,
        ))
        hop2.append(pltpu.make_async_remote_copy(
            src_ref=relay.at[piece], dst_ref=vrecv.at[piece], send_sem=ysem.at[2, n], recv_sem=ysem.at[3, n],
            device_id=to, device_id_type=MESH,
        ))
    for copy in hop1:
        copy.start()

    first = []
    for d in ORDER:
        peer = lax.rem(me + d, PEERS)
        copy = pltpu.make_async_remote_copy(
            src_ref=part.at[pl.ds(pl.multiple_of(lax.rem(peer, 8) * 16, 16), 16)],
            dst_ref=rx1.at[pl.ds((15 - d) * 16, 16)],
            send_sem=s1.at[d - 1], recv_sem=r1.at[d - 1],
            device_id={"vert": peer}, device_id_type=MESH,
        )
        copy.start()
        first.append(copy)


    quad_lane = lane >> 2

    def pack_cols(v, carry):
        acc = jnp.zeros((8, 128), F32)
        sides = acc
        for n in range(HALF):
            tile = v * HALF + n
            speed = speed_x(tile)
            right = speed > 0.0
            sides = jnp.where(quad_lane == n, speed, sides)
            sgn = jnp.where(right, 1.0, -1.0)
            for y in range(2):
                value = comp(tile, 0, y) + sgn * comp(tile, 1, y)
                for k, x in enumerate((value, comp(tile, 2, y))):
                    at = n * 4 + y * 2 + k
                    moved = jnp.where(right, pltpu.roll(x, (at + 1) % 128, 1), pltpu.roll(x, at, 1) if at else x)
                    acc = jnp.where(lane == at, moved, acc)
        xsend[pl.ds(pl.multiple_of(v * 8, 8), 8), :] = acc
        xside[pl.ds(pl.multiple_of(v * 8, 8), 8), :] = sides
        return carry

    lax.fori_loop(0, 2, pack_cols, 0)
    send_e = pltpu.make_async_remote_copy(
        src_ref=xsend, dst_ref=xleft, send_sem=xsem_s.at[0], recv_sem=xsem_r.at[0],
        device_id={"gx": east}, device_id_type=MESH,
    )
    send_w = pltpu.make_async_remote_copy(
        src_ref=xsend, dst_ref=xright, send_sem=xsem_s.at[1], recv_sem=xsem_r.at[1],
        device_id={"gx": west}, device_id_type=MESH,
    )
    send_e.start()
    send_w.start()

    for n in range(2):
        hop1[n].wait_recv()
        hop2[n].start()

    for copy in first:
        copy.wait_recv()
    chunk = pl.ds(pl.multiple_of(lax.rem(me, 8) * 16, 16), 16)
    total = part[chunk, :]
    for k in range(15):
        total = total + rx1[pl.ds(k * 16, 16), :]
    sumt[...] = total
    tot[chunk, :] = total
    core = lax.rem(me, 2)
    flip = 1 - 2 * core
    second = []
    for k, (chips, other) in enumerate(
        ((2 * flip, 0), (2 * flip, 1), (1, 0), (1, 1), (-1, 0), (-1, 1), (0, 1))
    ):
        copy = pltpu.make_async_remote_copy(
            src_ref=sumt, dst_ref=tot.at[chunk],
            send_sem=s2.at[k], recv_sem=r2.at[k],
            device_id={"vert": lax.rem(me + 2 * chips + other * flip + PEERS, PEERS)}, device_id_type=MESH,
        )
        copy.start()
        second.append(copy)

    for n in range(2, 4):
        hop1[n].wait_recv()
        hop2[n].start()

    load_w.wait()
    flags = walls_v[pl.ds(wall, 1), :].astype(F32)
    flag = jnp.broadcast_to(flags, (8, 128))

    def move(t, carry):
        for tile in (t, t + HALF):
            v_x = speed_x(tile)
            v_y = speed_y(tile)
            right = v_x > 0.0
            s_x = jnp.where(right, 1.0, -1.0)
            s_y = jnp.where(v_y > 0.0, 1.0, -1.0)
            a_x = jnp.abs(v_x)
            a_y = jnp.abs(v_y)
            inward = v_y * toward > 0.0
            cw, gxw, gyw = (comp(tile, k, wall) for k in range(3))
            ci, gxi, gyi = (comp(tile, k, inner) for k in range(3))
            fw = cw + s_y * gyw
            fi = ci + s_y * gyi
            u_w = (
                jnp.where(inward, flag * mirror(fw, low_pair), fi),
                jnp.where(inward, flag * mirror(gxw, low_pair), gxi),
            )
            u_i = (jnp.where(inward, fw, 0.0), jnp.where(inward, gxw, 0.0))
            outermost = lane == jnp.where(right, 0, 127)
            for y, c, g_x, g_y, f_y, (uy0, uy1) in (
                (wall, cw, gxw, gyw, fw, u_w),
                (inner, ci, gxi, gyi, fi, u_i),
            ):
                f_x = c + s_x * g_x
                ux0 = jnp.where(right, pltpu.roll(f_x, 1, 1), pltpu.roll(f_x, 127, 1))
                ux2 = jnp.where(right, pltpu.roll(g_y, 1, 1), pltpu.roll(g_y, 127, 1))
                ux0 = jnp.where(outermost, 0.0, ux0)
                ux2 = jnp.where(outermost, 0.0, ux2)
                c2 = c + c
                mean = a_x * (f_x - ux0) + a_y * (f_y - uy0) + c2
                rx = 3.0 * v_x * (f_x + ux0 - c2) + a_y * (g_x - uy1) + 2.0 * g_x
                ry = a_x * (g_y - ux2) + 3.0 * v_y * (f_y + uy0 - c2) + 2.0 * g_y
                for k, value in enumerate((mean, rx, ry)):
                    at = pl.multiple_of((tile * 6 + k * 2 + y) * 8, 8)
                    tb[pl.ds(at, 8), :] = value
        return carry

    lax.fori_loop(0, HALF, move, 0, unroll=2)

    send_e.wait_recv()
    send_w.wait_recv()

    def add_edges(v, carry):
        rows8 = pl.ds(pl.multiple_of(v * 8, 8), 8)
        came = jnp.where(xside[rows8, :] > 0.0, xleft[rows8, :], xright[rows8, :])
        for n in range(HALF):
            tile = v * HALF + n
            speed = speed_x(tile)
            speed = jnp.where(lane == jnp.where(speed > 0.0, 0, 127), speed, 0.0)
            a_x = jnp.abs(speed)
            for y in range(2):
                value, slope = (
                    jnp.broadcast_to(came[:, n * 4 + y * 2 + k : n * 4 + y * 2 + k + 1], (8, 128)) for k in range(2)
                )
                for k, term in enumerate((-a_x * value, 3.0 * speed * value, -a_x * slope)):
                    at = pl.ds(pl.multiple_of((tile * 6 + k * 2 + y) * 8, 8), 8)
                    tb[at, :] = tb[at, :] + term
        return carry

    lax.fori_loop(0, 2, add_edges, 0)

    for copy in second:
        copy.wait_recv()
    upper = sub >= 4
    q_of = lax.rem(sub, 4)
    xi = jnp.where(q_of >= 2, GAUSS, -GAUSS)
    eta = jnp.where(lax.rem(q_of, 2) == 1, GAUSS, -GAUSS)

    def moment(k):
        s, n = divmod(k, 10)
        coefs = []
        for j in range(6):
            c = s * 6 + j
            at = c * 8 + n if n < 8 else (12 + c // 4) * 8 + (c % 4) * 2 + n - 8
            coefs.append(jnp.broadcast_to(tot[pl.ds(at, 1), :], (8, 128)))
        a, b, c = (jnp.where(upper, coefs[2 * m + 1], coefs[2 * m]) for m in range(3))
        return a + xi * b + eta * c

    expo, fact = gauss_coefs([moment(k) for k in range(20)])
    for half, coefs in enumerate((expo, fact)):
        for k, x in enumerate(coefs):
            for n, piece in enumerate(split3(x)):
                for r in (k,) if k < 4 else (k, k + 6):
                    cs[pl.ds(half * 384 + n * 16 + r, 8, stride=48), :] = piece
    for i in range(8):
        csb[i, 0:48, 0:128] = cs[i * 48 : i * 48 + 48, :].astype(BF16)
        csb[i, 0:48, 128:256] = cs[384 + i * 48 : 384 + i * 48 + 48, :].astype(BF16)

    for copy in hop2:
        copy.wait_recv()

    def add_halo(t, carry):
        base = pl.multiple_of(t * 16, 16)
        near = [vrecv[pl.ds(base, 8), :], vrecv[pl.ds(base + 8, 8), :]]
        first_in = speed_y(t) * toward > 0.0
        for tile in (t, t + HALF):
            v_y = speed_y(tile)
            speed = jnp.where(v_y * toward > 0.0, 0.0, v_y)
            value, slope = near if tile is t else [jnp.where(first_in, f, mirror(f, low_pair)) for f in near]
            a_y = jnp.abs(speed)
            for k, term in enumerate((-a_y * value, -a_y * slope, 3.0 * speed * value)):
                at = pl.ds(pl.multiple_of((tile * 6 + k * 2 + inner) * 8, 8), 8)
                tb[at, :] = tb[at, :] + term
        return carry

    lax.fori_loop(0, HALF, add_halo, 0, unroll=4)

    for copy in first + second + hop1 + hop2 + [send_e, send_w]:
        copy.wait_send()


def collide(tb, mg, csb, out_hbm, eq, ob, osem):
    stores = []
    tiles = TILES // PARTS
    for n in range(PARTS):
        rows = slice(n * tiles * 8, (n + 1) * tiles * 8)
        for i in range(8):
            eq[i, rows, :] = jnp.dot(mg[rows, 0:48], csb[i, 0:48, :], preferred_element_type=F32)
        for t in range(n * tiles, (n + 1) * tiles):
            rows8 = slice(t * 8, t * 8 + 8)
            for y in range(2):
                g = [jnp.exp2(eq[y * 4 + q, rows8, 0:128]) * eq[y * 4 + q, rows8, 128:256] for q in range(4)]
                low = g[0] + g[1]
                high = g[2] + g[3]
                vals = (
                    low + high,
                    (3.0 * GAUSS) * (high - low),
                    (3.0 * GAUSS) * ((g[1] - g[0]) + (g[3] - g[2])),
                )
                for k in range(3):
                    at = (t * 6 + k * 2 + y) * 8
                    ob[pl.ds(t * 48 + k * 2 + y, 8, stride=6), :] = tb[at : at + 8, :] + vals[k]
        begin = n * tiles * 48
        size = min(tiles * 48, ROWS - begin)
        store = pltpu.make_async_copy(ob.at[pl.ds(begin, size)], out_hbm.at[pl.ds(begin, size)], osem.at[n])
        store.start()
        stores.append(store)
    for store in stores:
        store.wait()


def shards(state, tangent, orient, walls):
    hbm = pl.BlockSpec(memory_space=pltpu.HBM)
    vmem = pl.BlockSpec(memory_space=pltpu.VMEM)
    tb, mg, csb = pl.pallas_call(
        gather,
        out_shape=(
            pltpu.VMEM((PAD_ROWS, 128), F32),
            pltpu.VMEM((PAD, 128), BF16),
            pltpu.VMEM((8, 128, 256), BF16),
        ),
        in_specs=[hbm] * 4,
        out_specs=[vmem] * 3,
        scratch_shapes=[
            pltpu.VMEM((PAD_ROWS, 128), F32),
            pltpu.VMEM((PAD_ROWS, 128), F32),
            pltpu.VMEM((2, SLOTS), jnp.int32),
            pltpu.VMEM((2, PAD), F32),
            pltpu.VMEM((2, 128), jnp.int32),
            pltpu.VMEM((32, PAD), BF16),
            pltpu.VMEM((PAD, 256), F32),
            pltpu.VMEM((128, 128), F32),
            pltpu.VMEM((240, 128), F32),
            pltpu.VMEM((16, 128), F32),
            pltpu.VMEM((128, 128), F32),
            pltpu.VMEM((HALF * 16, 128), F32),
            pltpu.VMEM((HALF * 16, 128), F32),
            pltpu.VMEM((HALF * 16, 128), F32),
            pltpu.VMEM((16, 128), F32),
            pltpu.VMEM((16, 128), F32),
            pltpu.VMEM((16, 128), F32),
            pltpu.VMEM((16, 128), F32),
            pltpu.VMEM((16 * 48, 128), F32),
            pltpu.SemaphoreType.DMA((6,)),
            pltpu.SemaphoreType.DMA((15,)),
            pltpu.SemaphoreType.DMA((15,)),
            pltpu.SemaphoreType.DMA((15,)),
            pltpu.SemaphoreType.DMA((15,)),
            pltpu.SemaphoreType.DMA((4, 4)),
            pltpu.SemaphoreType.DMA((2,)),
            pltpu.SemaphoreType.DMA((2,)),
        ],
        compiler_params=pltpu.CompilerParams(
            collective_id=0, has_side_effects=True, vmem_limit_bytes=58 * 1024 * 1024
        ),
    )(
        state.reshape(ROWS, 128),
        tangent.reshape(ROWS, 128),
        orient.T,
        walls,
    )
    out = pl.pallas_call(
        collide,
        out_shape=jax.ShapeDtypeStruct((ROWS, 128), F32),
        in_specs=[vmem] * 3,
        out_specs=hbm,
        scratch_shapes=[
            pltpu.VMEM((8, PAD, 256), F32),
            pltpu.VMEM((PAD_ROWS, 128), F32),
            pltpu.SemaphoreType.DMA((PARTS,)),
        ],
        compiler_params=pltpu.CompilerParams(vmem_limit_bytes=16 * 1024 * 1024),
    )(tb, mg, csb)
    return out.reshape(SLOTS, 3, 2, 128)


def solution(mesh):
    placed = (
        P("vert", None, "gy", "gx"),
        P("vert", None, "gy", "gx"),
        P("vert", None),
        P(None, "gx"),
    )
    return jax.shard_map(
        shards, mesh=mesh, in_specs=placed, out_specs=P("vert", None, "gy", "gx"), check_vma=False
    )
```

```python
import functools
import math

import jax
import jax.numpy as jnp
from jax import lax
from jax.experimental import pallas as pl
from jax.experimental.pallas import tpu as pltpu
from jax.sharding import PartitionSpec as P

MESH = pl.DeviceIdType.MESH
F32 = jnp.float32
BF16 = jnp.bfloat16

SLOTS = 500
PAD = 512
TILES = PAD // 8
HALF = TILES // 2
ROWS = SLOTS * 6
PAD_ROWS = PAD * 6
GAUSS = 0.5773502691896258
LOG_TWO_PI = math.log(2.0 * math.pi)
LOG2E = math.log2(math.e)
DUOS = ((0, 0), (1, 1), (2, 2), (0, 1), (0, 2), (1, 2))
PEERS = 16
PARTS = 4
ORDER = (8, 7, 9, 6, 10, 5, 11, 4, 12, 3, 13, 2, 14, 1, 15)


def full(entries):
    rows = [[None] * 3 for _ in range(3)]
    for n, (a, b) in enumerate(DUOS):
        rows[a][b] = entries[n]
        rows[b][a] = entries[n]
    return rows


def gauss_coefs(mom):
    rho = mom[0]
    inv_rho = 1.0 / rho
    u = [mom[1 + a] * inv_rho for a in range(3)]
    sec = mom[4:10]
    theta = [sec[n] * inv_rho - u[a] * u[b] for n, (a, b) in enumerate(DUOS)]
    temp = (theta[0] + theta[1] + theta[2]) * (1.0 / 3.0)
    tn = [(1.5 * temp if a == b else 0.0) - 0.5 * theta[n] for n, (a, b) in enumerate(DUOS)]
    t = full(tn)
    cof = [
        t[1][1] * t[2][2] - t[1][2] * t[1][2],
        t[0][0] * t[2][2] - t[0][2] * t[0][2],
        t[0][0] * t[1][1] - t[0][1] * t[0][1],
        t[0][2] * t[1][2] - t[0][1] * t[2][2],
        t[0][1] * t[1][2] - t[0][2] * t[1][1],
        t[0][1] * t[0][2] - t[0][0] * t[1][2],
    ]
    det = t[0][0] * cof[0] + t[0][1] * cof[3] + t[0][2] * cof[4]
    inv_det = 1.0 / det
    inv = [c * inv_det for c in cof]
    log_pre = jnp.log(rho) - 1.5 * LOG_TWO_PI - 0.5 * jnp.log(det)
    drho = mom[10]
    du = [(mom[11 + a] - u[a] * drho) * inv_rho for a in range(3)]
    dlog = drho * inv_rho
    dtheta = [
        (mom[14 + n] - sec[n] * dlog) * inv_rho - (du[a] * u[b] + u[a] * du[b])
        for n, (a, b) in enumerate(DUOS)
    ]
    dtemp = (dtheta[0] + dtheta[1] + dtheta[2]) * (1.0 / 3.0)
    dtn = [(1.5 * dtemp if a == b else 0.0) - 0.5 * dtheta[n] for n, (a, b) in enumerate(DUOS)]
    A = full(inv)
    D = full(dtn)
    trace = sum(A[a][b] * D[b][a] for a in range(3) for b in range(3))
    shift = dlog - 0.5 * trace
    w = [A[a][0] * du[0] + A[a][1] * du[1] + A[a][2] * du[2] for a in range(3)]
    AD = [[A[a][0] * D[0][c] + A[a][1] * D[1][c] + A[a][2] * D[2][c] for c in range(3)] for a in range(3)]
    curve = [AD[a][0] * A[0][b] + AD[a][1] * A[1][b] + AD[a][2] * A[2][b] for a, b in DUOS]
    B = full(curve)
    au = [A[a][0] * u[0] + A[a][1] * u[1] + A[a][2] * u[2] for a in range(3)]
    bu = [B[a][0] * u[0] + B[a][1] * u[1] + B[a][2] * u[2] for a in range(3)]
    e0 = log_pre - 0.5 * (u[0] * au[0] + u[1] * au[1] + u[2] * au[2])
    expo = [e0] + au + [-0.5 * inv[n] if n < 3 else -inv[n] for n in range(6)]
    q0 = shift - (u[0] * w[0] + u[1] * w[1] + u[2] * w[2]) + 0.5 * (u[0] * bu[0] + u[1] * bu[1] + u[2] * bu[2])
    fact = [q0] + [w[a] - bu[a] for a in range(3)] + [0.5 * curve[n] if n < 3 else curve[n] for n in range(6)]
    return [x * LOG2E for x in expo], [x * -0.5 for x in fact]


def split3(x):
    hi = x.astype(BF16).astype(F32)
    r = x - hi
    mid = r.astype(BF16).astype(F32)
    return hi, mid, r - mid


def mirror(x, low_pair):
    return jnp.where(low_pair, pltpu.roll(x, 6, 0), pltpu.roll(x, 2, 0))


def gather(
    state_hbm, tan_hbm, orient_hbm, walls_hbm, tb, mg, csb,
    xs, xt, orient_v, bits, walls_v, ml, vxy, part, rx1, sumt, tot,
    vsend, relay, vrecv, xsend, xside, xleft, xright, cs,
    lsem, s1, r1, s2, r2, ysem, xsem_s, xsem_r,
):
    me = lax.axis_index("vert")
    gx = lax.axis_index("gx")
    gy = lax.axis_index("gy")
    wall = gy
    inner = 1 - gy
    load_t, load_s = (
        [
            pltpu.make_async_copy(
                hbm.at[pl.ds(k * 1536, size)], ref.at[pl.ds(k * 1536, size)], lsem.at[2 * n + k]
            )
            for k, size in enumerate((1536, ROWS - 1536))
        ]
        for n, (hbm, ref) in enumerate(((tan_hbm, xt), (state_hbm, xs)))
    )
    load_o = pltpu.make_async_copy(orient_hbm, orient_v, lsem.at[4])
    load_w = pltpu.make_async_copy(walls_hbm, walls_v, lsem.at[5])
    load_o.start()
    for copy in load_t + load_s:
        copy.start()
    load_w.start()

    barrier = pltpu.get_barrier_semaphore()
    for d in ORDER:
        pl.semaphore_signal(barrier, inc=1, device_id={"vert": lax.rem(me + d, PEERS)}, device_id_type=MESH)
    odd = lax.rem(gx, 2)
    side = gx + 1 - 2 * odd
    plus = {"gx": side, "gy": lax.rem(gy + odd, 2)}
    minus = {"gx": side, "gy": lax.rem(gy + odd + 1, 2)}
    pl.semaphore_signal(barrier, inc=1, device_id={"gx": side, "gy": inner}, device_id_type=MESH)
    east = lax.rem(gx + 1, 8)
    west = lax.rem(gx + 7, 8)
    pl.semaphore_signal(barrier, inc=1, device_id={"gx": east}, device_id_type=MESH)
    pl.semaphore_signal(barrier, inc=1, device_id={"gx": west}, device_id_type=MESH)

    zeros_tail = jnp.zeros((PAD_ROWS - ROWS, 128), F32)
    xs[pl.ds(ROWS, PAD_ROWS - ROWS), :] = zeros_tail
    xt[pl.ds(ROWS, PAD_ROWS - ROWS), :] = zeros_tail
    bits[...] = jnp.zeros((2, PAD), F32)
    load_o.wait()
    bits[:, 0:SLOTS] = orient_v[...].astype(F32)
    row = lax.broadcasted_iota(jnp.int32, (8, PAD), 0)
    slot = (lax.broadcasted_iota(jnp.int32, (8, PAD), 1) + me * SLOTS).astype(F32) + 0.5
    by40 = jnp.floor(slot * (1.0 / 40.0))
    by400 = jnp.floor(slot * (1.0 / 400.0))
    by4 = jnp.floor(slot * 0.25)
    sx = jnp.broadcast_to(bits[0:1, :], (8, PAD)) * 2.0 - 1.0
    sy = jnp.broadcast_to(bits[1:2, :], (8, PAD)) * 2.0 - 1.0
    vx = sx * (by40 - 10.0 * by400 + 0.5) * 0.5
    vy = sy * (by4 - 10.0 * by40 + 0.5) * 0.5
    vz = (by400 - 9.5) * 0.5
    quad = [vx * vx, vy * vy, vz * vz, vx * vy, vx * vz, vy * vz]
    qhi = [q.astype(BF16).astype(F32) for q in quad]
    qlo = [q - h for q, h in zip(quad, qhi)]
    lin = [jnp.ones((8, PAD), F32), vx, vy, vz]
    zero = jnp.zeros((8, PAD), F32)

    def pick(values):
        out = values[0]
        for k in range(1, 8):
            out = jnp.where(row == k, values[k], out)
        return out

    head = pick(lin + qhi[:4])
    tail = pick(qhi[4:] + qlo)
    lows = pick([zero] * 4 + qlo[:4])
    even = lax.rem(row, 2) == 0
    pair_hi = jnp.where(even, qhi[4], qhi[5])
    pair_lo = jnp.where(even, qlo[4], qlo[5])
    ml[...] = (jnp.concatenate([head, lows, pair_hi, pair_lo], axis=0) * 0.125).astype(BF16)
    table = jnp.concatenate([head, tail] * 3 + [zero] * 10, axis=0)
    mg[...] = jnp.transpose(table).astype(BF16)
    krow = lax.broadcasted_iota(jnp.int32, (128, 256), 0)
    kcol = lax.broadcasted_iota(jnp.int32, (128, 256), 1)
    choose = jnp.where(krow == 1 + (kcol >> 7), 1.0, 0.0).astype(BF16)
    vxy[...] = jnp.dot(mg[...], choose, preferred_element_type=F32)
    csb[...] = jnp.zeros(csb.shape, BF16)

    sub = lax.broadcasted_iota(jnp.int32, (8, 128), 0)
    lane = lax.broadcasted_iota(jnp.int32, (8, 128), 1)
    low_pair = lax.rem(sub, 4) < 2
    toward = (1 - 2 * gy).astype(F32)

    def comp(tile, coef, y):
        return xt[pl.ds(tile * 48 + coef * 2 + y, 8, stride=6), :]

    def speed_x(tile):
        return vxy[pl.ds(pl.multiple_of(tile * 8, 8), 8), 0:128]

    def speed_y(tile):
        return vxy[pl.ds(pl.multiple_of(tile * 8, 8), 8), 128:256]


    group = sub // 2
    packed = [None] * 3

    def sums(ref, first, loads):
        accs = [None] * 3
        for k in range(2):
            loads[k].wait()
            for p in range(3):
                pair = [ref[pl.ds(k * 1536 + 2 * p + h, 256, stride=6), :] for h in range(2)]
                for piece in split3(jnp.concatenate(pair, axis=1)):
                    got = jnp.dot(ml[:, k * 256 : k * 256 + 256], piece.astype(BF16), preferred_element_type=F32)
                    accs[p] = got if accs[p] is None else accs[p] + got
        for p, acc in enumerate(accs):
            for h in range(2):
                c = first + 2 * p + h
                cols = slice(h * 128, h * 128 + 128)
                part[pl.ds(c * 8, 8), :] = acc[0:8, cols] + acc[8:16, cols]
                extra = acc[16:24, cols] + acc[24:32, cols]
                old = packed[c // 4]
                packed[c // 4] = extra if old is None else jnp.where(group == c % 4, extra, old)

    sums(xt, 6, load_t)

    def pack_rows(t, carry):
        traces = []
        for tile in (t, t + HALF):
            v = speed_y(tile)
            sgn = jnp.where(v > 0.0, 1.0, -1.0)
            value = comp(tile, 0, inner) + sgn * comp(tile, 2, inner)
            traces.append((v * toward > 0.0, value, comp(tile, 1, inner)))
        (in0, val0, slo0), (in1, val1, slo1) = traces
        base = pl.multiple_of(t * 16, 16)
        vsend[pl.ds(base, 8), :] = jnp.where(in0, val0, jnp.where(in1, val1, mirror(val1, low_pair)))
        vsend[pl.ds(base + 8, 8), :] = jnp.where(in0, slo0, jnp.where(in1, slo1, mirror(slo1, low_pair)))
        return carry

    lax.fori_loop(0, HALF, pack_rows, 0, unroll=4)

    sums(xs, 0, load_s)
    for i in range(3):
        part[pl.ds((12 + i) * 8, 8), :] = packed[i]
    part[pl.ds(120, 8), :] = jnp.zeros((8, 128), F32)

    pl.semaphore_wait(barrier, PEERS + 2)

    hop1 = []
    hop2 = []
    for n, (to, begin, size) in enumerate(
        ((plus, 0, 192), (minus, 192, 192), (plus, 384, 64), (minus, 448, 64))
    ):
        piece = pl.ds(begin, size)
        hop1.append(pltpu.make_async_remote_copy(
            src_ref=vsend.at[piece], dst_ref=relay.at[piece], send_sem=ysem.at[0, n], recv_sem=ysem.at[1, n],
            device_id=to, device_id_type=MESH,
        ))
        hop2.append(pltpu.make_async_remote_copy(
            src_ref=relay.at[piece], dst_ref=vrecv.at[piece], send_sem=ysem.at[2, n], recv_sem=ysem.at[3, n],
            device_id=to, device_id_type=MESH,
        ))
    for copy in hop1:
        copy.start()

    first = []
    for d in ORDER:
        peer = lax.rem(me + d, PEERS)
        copy = pltpu.make_async_remote_copy(
            src_ref=part.at[pl.ds(pl.multiple_of(lax.rem(peer, 8) * 16, 16), 16)],
            dst_ref=rx1.at[pl.ds((15 - d) * 16, 16)],
            send_sem=s1.at[d - 1], recv_sem=r1.at[d - 1],
            device_id={"vert": peer}, device_id_type=MESH,
        )
        copy.start()
        first.append(copy)


    quad_lane = lane >> 2

    def pack_cols(v, carry):
        acc = jnp.zeros((8, 128), F32)
        sides = acc
        for n in range(HALF):
            tile = v * HALF + n
            speed = speed_x(tile)
            right = speed > 0.0
            sides = jnp.where(quad_lane == n, speed, sides)
            sgn = jnp.where(right, 1.0, -1.0)
            for y in range(2):
                value = comp(tile, 0, y) + sgn * comp(tile, 1, y)
                for k, x in enumerate((value, comp(tile, 2, y))):
                    at = n * 4 + y * 2 + k
                    moved = jnp.where(right, pltpu.roll(x, (at + 1) % 128, 1), pltpu.roll(x, at, 1) if at else x)
                    acc = jnp.where(lane == at, moved, acc)
        xsend[pl.ds(pl.multiple_of(v * 8, 8), 8), :] = acc
        xside[pl.ds(pl.multiple_of(v * 8, 8), 8), :] = sides
        return carry

    lax.fori_loop(0, 2, pack_cols, 0)
    send_e = pltpu.make_async_remote_copy(
        src_ref=xsend, dst_ref=xleft, send_sem=xsem_s.at[0], recv_sem=xsem_r.at[0],
        device_id={"gx": east}, device_id_type=MESH,
    )
    send_w = pltpu.make_async_remote_copy(
        src_ref=xsend, dst_ref=xright, send_sem=xsem_s.at[1], recv_sem=xsem_r.at[1],
        device_id={"gx": west}, device_id_type=MESH,
    )
    send_e.start()
    send_w.start()

    for n in range(2):
        hop1[n].wait_recv()
        hop2[n].start()

    for copy in first:
        copy.wait_recv()
    chunk = pl.ds(pl.multiple_of(lax.rem(me, 8) * 16, 16), 16)
    total = part[chunk, :]
    for k in range(15):
        total = total + rx1[pl.ds(k * 16, 16), :]
    sumt[...] = total
    tot[chunk, :] = total
    core = lax.rem(me, 2)
    flip = 1 - 2 * core
    second = []
    for k, (chips, other) in enumerate(
        ((2 * flip, 0), (2 * flip, 1), (1, 0), (1, 1), (-1, 0), (-1, 1), (0, 1))
    ):
        copy = pltpu.make_async_remote_copy(
            src_ref=sumt, dst_ref=tot.at[chunk],
            send_sem=s2.at[k], recv_sem=r2.at[k],
            device_id={"vert": lax.rem(me + 2 * chips + other * flip + PEERS, PEERS)}, device_id_type=MESH,
        )
        copy.start()
        second.append(copy)

    for n in range(2, 4):
        hop1[n].wait_recv()
        hop2[n].start()

    load_w.wait()
    flags = walls_v[pl.ds(wall, 1), :].astype(F32)
    flag = jnp.broadcast_to(flags, (8, 128))

    def move(t, carry):
        for tile in (t, t + HALF):
            v_x = speed_x(tile)
            v_y = speed_y(tile)
            right = v_x > 0.0
            s_x = jnp.where(right, 1.0, -1.0)
            s_y = jnp.where(v_y > 0.0, 1.0, -1.0)
            a_x = jnp.abs(v_x)
            a_y = jnp.abs(v_y)
            inward = v_y * toward > 0.0
            cw, gxw, gyw = (comp(tile, k, wall) for k in range(3))
            ci, gxi, gyi = (comp(tile, k, inner) for k in range(3))
            fw = cw + s_y * gyw
            fi = ci + s_y * gyi
            u_w = (
                jnp.where(inward, flag * mirror(fw, low_pair), fi),
                jnp.where(inward, flag * mirror(gxw, low_pair), gxi),
            )
            u_i = (jnp.where(inward, fw, 0.0), jnp.where(inward, gxw, 0.0))
            outermost = lane == jnp.where(right, 0, 127)
            for y, c, g_x, g_y, f_y, (uy0, uy1) in (
                (wall, cw, gxw, gyw, fw, u_w),
                (inner, ci, gxi, gyi, fi, u_i),
            ):
                f_x = c + s_x * g_x
                ux0 = jnp.where(right, pltpu.roll(f_x, 1, 1), pltpu.roll(f_x, 127, 1))
                ux2 = jnp.where(right, pltpu.roll(g_y, 1, 1), pltpu.roll(g_y, 127, 1))
                ux0 = jnp.where(outermost, 0.0, ux0)
                ux2 = jnp.where(outermost, 0.0, ux2)
                c2 = c + c
                mean = a_x * (f_x - ux0) + a_y * (f_y - uy0) + c2
                rx = 3.0 * v_x * (f_x + ux0 - c2) + a_y * (g_x - uy1) + 2.0 * g_x
                ry = a_x * (g_y - ux2) + 3.0 * v_y * (f_y + uy0 - c2) + 2.0 * g_y
                for k, value in enumerate((mean, rx, ry)):
                    at = pl.multiple_of((tile * 6 + k * 2 + y) * 8, 8)
                    tb[pl.ds(at, 8), :] = value
        return carry

    lax.fori_loop(0, HALF, move, 0, unroll=2)

    send_e.wait_recv()
    send_w.wait_recv()

    def add_edges(v, carry):
        rows8 = pl.ds(pl.multiple_of(v * 8, 8), 8)
        came = jnp.where(xside[rows8, :] > 0.0, xleft[rows8, :], xright[rows8, :])
        for n in range(HALF):
            tile = v * HALF + n
            speed = speed_x(tile)
            speed = jnp.where(lane == jnp.where(speed > 0.0, 0, 127), speed, 0.0)
            a_x = jnp.abs(speed)
            for y in range(2):
                value, slope = (
                    jnp.broadcast_to(came[:, n * 4 + y * 2 + k : n * 4 + y * 2 + k + 1], (8, 128)) for k in range(2)
                )
                for k, term in enumerate((-a_x * value, 3.0 * speed * value, -a_x * slope)):
                    at = pl.ds(pl.multiple_of((tile * 6 + k * 2 + y) * 8, 8), 8)
                    tb[at, :] = tb[at, :] + term
        return carry

    lax.fori_loop(0, 2, add_edges, 0)

    for copy in second:
        copy.wait_recv()
    upper = sub >= 4
    q_of = lax.rem(sub, 4)
    xi = jnp.where(q_of >= 2, GAUSS, -GAUSS)
    eta = jnp.where(lax.rem(q_of, 2) == 1, GAUSS, -GAUSS)

    def moment(k):
        s, n = divmod(k, 10)
        coefs = []
        for j in range(6):
            c = s * 6 + j
            at = c * 8 + n if n < 8 else (12 + c // 4) * 8 + (c % 4) * 2 + n - 8
            coefs.append(jnp.broadcast_to(tot[pl.ds(at, 1), :], (8, 128)))
        a, b, c = (jnp.where(upper, coefs[2 * m + 1], coefs[2 * m]) for m in range(3))
        return a + xi * b + eta * c

    expo, fact = gauss_coefs([moment(k) for k in range(20)])
    for half, coefs in enumerate((expo, fact)):
        for k, x in enumerate(coefs):
            for n, piece in enumerate(split3(x)):
                for r in (k,) if k < 4 else (k, k + 6):
                    cs[pl.ds(half * 384 + n * 16 + r, 8, stride=48), :] = piece
    for i in range(8):
        csb[i, 0:48, 0:128] = cs[i * 48 : i * 48 + 48, :].astype(BF16)
        csb[i, 0:48, 128:256] = cs[384 + i * 48 : 384 + i * 48 + 48, :].astype(BF16)

    for copy in hop2:
        copy.wait_recv()

    def add_halo(t, carry):
        base = pl.multiple_of(t * 16, 16)
        near = [vrecv[pl.ds(base, 8), :], vrecv[pl.ds(base + 8, 8), :]]
        first_in = speed_y(t) * toward > 0.0
        for tile in (t, t + HALF):
            v_y = speed_y(tile)
            speed = jnp.where(v_y * toward > 0.0, 0.0, v_y)
            value, slope = near if tile is t else [jnp.where(first_in, f, mirror(f, low_pair)) for f in near]
            a_y = jnp.abs(speed)
            for k, term in enumerate((-a_y * value, -a_y * slope, 3.0 * speed * value)):
                at = pl.ds(pl.multiple_of((tile * 6 + k * 2 + inner) * 8, 8), 8)
                tb[at, :] = tb[at, :] + term
        return carry

    lax.fori_loop(0, HALF, add_halo, 0, unroll=4)

    for copy in first + second + hop1 + hop2 + [send_e, send_w]:
        copy.wait_send()


def collide(tb, mg, csb, out_hbm, eq, ob, osem):
    stores = []
    tiles = TILES // PARTS
    for n in range(PARTS):
        rows = slice(n * tiles * 8, (n + 1) * tiles * 8)
        for i in range(8):
            eq[i, rows, :] = jnp.dot(mg[rows, 0:48], csb[i, 0:48, :], preferred_element_type=F32)
        for t in range(n * tiles, (n + 1) * tiles):
            rows8 = slice(t * 8, t * 8 + 8)
            for y in range(2):
                g = [jnp.exp2(eq[y * 4 + q, rows8, 0:128]) * eq[y * 4 + q, rows8, 128:256] for q in range(4)]
                low = g[0] + g[1]
                high = g[2] + g[3]
                vals = (
                    low + high,
                    (3.0 * GAUSS) * (high - low),
                    (3.0 * GAUSS) * ((g[1] - g[0]) + (g[3] - g[2])),
                )
                for k in range(3):
                    at = (t * 6 + k * 2 + y) * 8
                    ob[pl.ds(t * 48 + k * 2 + y, 8, stride=6), :] = tb[at : at + 8, :] + vals[k]
        begin = n * tiles * 48
        size = min(tiles * 48, ROWS - begin)
        store = pltpu.make_async_copy(ob.at[pl.ds(begin, size)], out_hbm.at[pl.ds(begin, size)], osem.at[n])
        store.start()
        stores.append(store)
    for store in stores:
        store.wait()


def shards(state, tangent, orient, walls):
    hbm = pl.BlockSpec(memory_space=pltpu.HBM)
    vmem = pl.BlockSpec(memory_space=pltpu.VMEM)
    tb, mg, csb = pl.pallas_call(
        gather,
        out_shape=(
            pltpu.VMEM((PAD_ROWS, 128), F32),
            pltpu.VMEM((PAD, 128), BF16),
            pltpu.VMEM((8, 128, 256), BF16),
        ),
        in_specs=[hbm] * 4,
        out_specs=[vmem] * 3,
        scratch_shapes=[
            pltpu.VMEM((PAD_ROWS, 128), F32),
            pltpu.VMEM((PAD_ROWS, 128), F32),
            pltpu.VMEM((2, SLOTS), jnp.int32),
            pltpu.VMEM((2, PAD), F32),
            pltpu.VMEM((2, 128), jnp.int32),
            pltpu.VMEM((32, PAD), BF16),
            pltpu.VMEM((PAD, 256), F32),
            pltpu.VMEM((128, 128), F32),
            pltpu.VMEM((240, 128), F32),
            pltpu.VMEM((16, 128), F32),
            pltpu.VMEM((128, 128), F32),
            pltpu.VMEM((HALF * 16, 128), F32),
            pltpu.VMEM((HALF * 16, 128), F32),
            pltpu.VMEM((HALF * 16, 128), F32),
            pltpu.VMEM((16, 128), F32),
            pltpu.VMEM((16, 128), F32),
            pltpu.VMEM((16, 128), F32),
            pltpu.VMEM((16, 128), F32),
            pltpu.VMEM((16 * 48, 128), F32),
            pltpu.SemaphoreType.DMA((6,)),
            pltpu.SemaphoreType.DMA((15,)),
            pltpu.SemaphoreType.DMA((15,)),
            pltpu.SemaphoreType.DMA((15,)),
            pltpu.SemaphoreType.DMA((15,)),
            pltpu.SemaphoreType.DMA((4, 4)),
            pltpu.SemaphoreType.DMA((2,)),
            pltpu.SemaphoreType.DMA((2,)),
        ],
        compiler_params=pltpu.CompilerParams(
            collective_id=0, has_side_effects=True, vmem_limit_bytes=58 * 1024 * 1024
        ),
    )(
        state.reshape(ROWS, 128),
        tangent.reshape(ROWS, 128),
        orient.T,
        walls,
    )
    out = pl.pallas_call(
        collide,
        out_shape=jax.ShapeDtypeStruct((ROWS, 128), F32),
        in_specs=[vmem] * 3,
        out_specs=hbm,
        scratch_shapes=[
            pltpu.VMEM((8, PAD, 256), F32),
            pltpu.VMEM((PAD_ROWS, 128), F32),
            pltpu.SemaphoreType.DMA((PARTS,)),
        ],
        compiler_params=pltpu.CompilerParams(vmem_limit_bytes=16 * 1024 * 1024),
    )(tb, mg, csb)
    return out.reshape(SLOTS, 3, 2, 128)


def solution(mesh):
    placed = (
        P("vert", None, "gy", "gx"),
        P("vert", None, "gy", "gx"),
        P("vert", None),
        P(None, "gx"),
    )
    return jax.shard_map(
        shards, mesh=mesh, in_specs=placed, out_specs=P("vert", None, "gy", "gx"), check_vma=False
    )
```
